32 devices in a mesh: row: 4 (over z), col: 8 (over y, x, core).
Axes of the slice: x: 2, y: 2, z: 4, core: 2. Of those that a mesh axis runs over, the one named last changes fastest.
Arguments:
- scans: float32 [4096, 4, 8, 128], P(('row', 'col')), may hold values from -6 to 6
- dest: int32 [4096, 1], P(('row', 'col')), may hold values from 0 to 31; in each aligned block of 128 rows (0 to 127, 128 to 255, ...) at most 8 rows name the same one
- offsets: int32 [4096], P(('row', 'col')), may hold values from 0 to 252
- profile_index: int32 [4096], P(('row', 'col')), may hold values from 0 to 15
- profiles: float32 [16, 4, 128], replicated, may hold values from 0.1 to 1.5
- embed_weight: bfloat16 [512, 1024], replicated, may hold values from -0.25 to 0.25
- attn_gain: float32 [2, 1024], replicated, may hold values from 0.1 to 1.9
- qkv_weight: bfloat16 [2, 1024, 3072], replicated, may hold values from -3 to 3
- out_weight: bfloat16 [2, 1024, 1024], replicated, may hold values from -0.1875 to 0.1875
Outputs:
- tokens: bfloat16 [128, 128, 1024], P('row', 'col')
The draws below stay inside these ranges and needn't reach their ends.
Inputs may be any that keep to these rules, and one draw needn't show every extreme that they name: dest[b, 0] is the tile of block b, numbered 8 * tile row + tile column; of the 128 blocks of one device at most 8 go to any one tile.
All inputs are finite; a program needn't handle non-finite values.
Results may differ from the reference program's by a relative error of at most 0.012.
Values may be sent and summed in bfloat16 or wider, within the bound.
A program may use at most 128 MiB of HBM per device.

```python
import math
import jax
import jax.numpy as jnp
import numpy as np
from jax import lax

C = 8
D = 1024
HEADS = 16
RADIUS = 4
LAYERS = 2
BR = 4
NWT = 16
TOK_H = 32
TOK_W = 16
SCANS = 128
CAP = 8
NBLK = 4096
N_ROW = 4
N_COL = 8
DEVICES = 32


def draw_qkv_weight(key, part):
    drawn = jnp.clip(jax.random.normal(key, (LAYERS, D, 3 * D), jnp.float32), -4.0, 4.0) * D ** (-0.5)
    return drawn.astype(jnp.bfloat16)


def plant(entries, own_key, smallest, high):
    spot = [jax.random.randint(jax.random.fold_in(own_key, axis), (), 0, length) for axis, length in enumerate(entries.shape)]
    longest = entries.shape.index(max(entries.shape))
    neighbour = spot[:longest] + [(spot[longest] + 1) % entries.shape[longest]] + spot[longest + 1:]
    return entries.at[tuple(spot)].set(smallest).at[tuple(neighbour)].set(high)


def block_levels(stream_key, shape, cuts, smallest, top_value):
    loudness, own = 1.0, jax.random.fold_in(stream_key, 6)
    for dim, parts in cuts:
        steps = jnp.exp(jax.random.uniform(jax.random.fold_in(own, dim), (parts,), jnp.float32, smallest / len(cuts), top_value / len(cuts)))
        loudness = loudness * jnp.repeat(steps, shape[dim] // parts).reshape([-1 if axis == dim else 1 for axis in range(len(shape))])
    return loudness


def routed_block(own_key, own, number, rows, amount, top, bound, skew):
    ranking = jax.random.permutation(own_key, amount)
    heavy_load, common = portions_of(amount, rows * top, bound, skew, True), portions_of(amount, rows * top, bound, skew, False)
    places = jnp.arange(amount)

    def named(lengths, rotation):
        used = int((lengths > 0).sum())
        fixed = max(1, used // 4)
        moved = fixed + (places - fixed + rotation * (used - fixed)) % max(1, amount - fixed)
        return jnp.zeros((amount,), jnp.int32).at[ranking[jnp.where(places < fixed, places, moved)]].set(jnp.asarray(lengths, jnp.int32))

    lengths = jnp.where(number % 4 == 0, named(heavy_load, number // 4), named(common, number - number // 4 - 1))
    mixed = jax.random.permutation(jax.random.fold_in(own, 3), amount)
    giver, taker = mixed[0:amount // 2 * 2:2], mixed[1:amount // 2 * 2:2]
    slack = jnp.minimum(lengths[giver] - 1, bound - lengths[taker]) // 2
    slack = jnp.where((giver == ranking[0]) | (taker == ranking[0]) | (lengths[taker] == 0), 0, jnp.maximum(slack, 0))
    moved = jax.random.randint(jax.random.fold_in(own, 4), (amount // 2,), 0, 1 << 20) % (slack + 1)
    lengths = lengths.at[giver].add(-moved).at[taker].add(moved)
    items = jnp.searchsorted(jnp.cumsum(lengths), jnp.arange(rows * top), side="right").astype(jnp.int32)
    table = items.reshape(top, rows).T
    table = table[jax.random.permutation(jax.random.fold_in(own, 1), rows)]
    rotation = jax.random.randint(jax.random.fold_in(own, 2), (rows, 1), 0, top)
    return jnp.take_along_axis(table, (jnp.arange(top)[None, :] + rotation) % top, axis=1)


def portions_of(number_of, total, limit, slope, full):
    weights = [(1 << 20) // math.isqrt(grade ** slope) + 1 for grade in range(1, number_of + 1)]
    largest = limit if full else min(limit, max(-(-total // number_of), total * weights[0] // sum(weights)))
    least = 1 if total - largest >= number_of - 1 else 0
    holding, surplus = [largest] + [least] * (number_of - 1), total - largest - least * (number_of - 1)
    while surplus > 0:
        movable = [i for i in range(1, number_of) if holding[i] < largest] or [i for i in range(1, number_of) if holding[i] < limit]
        pool, budget = sum([weights[i] for i in movable]), surplus
        for i in movable:
            extra = min(limit - holding[i], max(1, budget * weights[i] // pool), surplus)
            holding[i] = holding[i] + extra
            surplus = surplus - extra
    return np.array(holding)


def noise(stream_key, shape, deviation, most, pieces=(), kind=jnp.bfloat16):
    array = jax.random.normal(stream_key, shape, jnp.float32) * deviation
    if len(pieces) > 0:
        array = block_levels(stream_key, shape, pieces, -0.22, 0.18) * array
    return jnp.clip(array, min=-most, max=most).astype(kind)


def setup_inputs(seed: int = 0) -> dict:
    arg_keys = jax.random.split(jax.random.key(seed), 10)
    scans = noise(arg_keys[0], (NBLK, BR, C, 8 * TOK_W), 1.0, 6.0, ((0, 32),), jnp.float32)
    dest_keys = jax.random.split(jax.random.fold_in(arg_keys[1], 1), NBLK // SCANS)
    dest_turns = jax.random.permutation(jax.random.fold_in(arg_keys[1], 3), NBLK // SCANS)
    dest = jax.vmap(lambda own, number: routed_block(jax.random.fold_in(arg_keys[1], 2), own, number, SCANS, DEVICES, 1, CAP, 2))(dest_keys, dest_turns).reshape((NBLK, 1))
    offsets = plant(jax.random.randint(arg_keys[2], (NBLK,), 0, 8 * TOK_H - BR + 1), jax.random.fold_in(arg_keys[2], 1), 0, 8 * TOK_H - BR).astype(jnp.int32)
    profile_index = plant(jax.random.randint(arg_keys[3], (NBLK,), 0, NWT), jax.random.fold_in(arg_keys[3], 1), 0, NWT - 1).astype(jnp.int32)
    profiles = jnp.clip(jnp.exp(jax.random.uniform(arg_keys[4], (NWT, BR, 8 * TOK_W), jnp.float32, math.log(0.1), math.log(1.5))), 0.1, 1.5)
    embed_weight = noise(arg_keys[5], (64 * C, D), (64 * C) ** -0.5, 0.25)
    attn_gain = jnp.clip(1.0 + 0.18 * jax.random.normal(arg_keys[6], (LAYERS, D), jnp.float32), 0.1, 1.9)
    qkv_weight = draw_qkv_weight(jax.random.fold_in(arg_keys[9], 71), 0)
    out_weight = noise(arg_keys[8], (LAYERS, D, D), D ** -0.5, 0.1875)
    return dict(scans=scans, dest=dest, offsets=offsets, profile_index=profile_index, profiles=profiles, embed_weight=embed_weight, attn_gain=attn_gain, qkv_weight=qkv_weight, out_weight=out_weight)


def normed(stream, gain_row):
    centre = lax.optimization_barrier(jnp.mean(stream, -1, keepdims=True))
    spread = lax.optimization_barrier(jnp.mean(jnp.square(stream - centre), -1, keepdims=True))
    return ((stream - centre) * lax.rsqrt(spread + 1e-05) * gain_row).astype(jnp.bfloat16)

def reference(scans, dest, offsets, profile_index, profiles, embed_weight, attn_gain, qkv_weight, out_weight):
    tile_rows = TOK_H * 8
    tile_cols = TOK_W * 8
    grid_h = TOK_H * N_ROW
    grid_w = TOK_W * N_COL
    pixel_cols = grid_w * 8
    pixel_total = grid_h * 8 * pixel_cols
    targets = dest[:, 0]
    block_weight = profiles[profile_index]
    weighted = scans * block_weight[:, :, None, :]
    top_row = (targets // N_COL * tile_rows + offsets).astype(jnp.int32)
    left_col = (targets % N_COL * tile_cols).astype(jnp.int32)
    pix_rows = top_row[:, None] + jnp.arange(BR, dtype=jnp.int32)[None, :]
    pix_cols = left_col[:, None] + jnp.arange(tile_cols, dtype=jnp.int32)[None, :]
    flat_idx = (pix_rows[:, :, None] * pixel_cols + pix_cols[:, None, :]).reshape(-1).astype(jnp.int32)
    weighted_rows = weighted.transpose(0, 1, 3, 2).reshape(-1, C)
    numerator = jax.ops.segment_sum(weighted_rows, flat_idx, num_segments=pixel_total)
    numerator = numerator.reshape(grid_h * 8, pixel_cols, C).transpose(0, 2, 1)
    weight_sum = jax.ops.segment_sum(block_weight.reshape(-1), flat_idx, num_segments=pixel_total)
    weight_sum = weight_sum.reshape(grid_h * 8, pixel_cols)
    merged = (numerator / (1.0 + weight_sum[:, None, :])).astype(jnp.bfloat16)
    patches = merged.reshape(grid_h, 8, C, grid_w, 8).transpose(0, 3, 2, 1, 4).reshape(grid_h * grid_w, C * 64)
    stream = jnp.dot(patches, embed_weight, preferred_element_type=jnp.float32)
    head_dim = D // HEADS
    score_scale = head_dim ** (-0.5)
    window = 2 * RADIUS + 1
    inside_grid = jnp.pad(jnp.ones((grid_h, grid_w), jnp.float32), RADIUS)
    padding = ((RADIUS, RADIUS), (RADIUS, RADIUS), (0, 0), (0, 0))
    for layer_idx in range(LAYERS):
        inputs = normed(stream, attn_gain[layer_idx])
        projected = jnp.dot(inputs, qkv_weight[layer_idx], preferred_element_type=jnp.float32).astype(jnp.bfloat16)
        queries = projected[:, :D].reshape(grid_h, grid_w, HEADS, head_dim)
        key_heads = jnp.pad(projected[:, D:2 * D].reshape(grid_h, grid_w, HEADS, head_dim), padding)
        values = jnp.pad(projected[:, 2 * D:].reshape(grid_h, grid_w, HEADS, head_dim), padding)

        def one_row(row_idx):
            query_row = lax.dynamic_index_in_dim(queries, row_idx, 0, keepdims=False).astype(jnp.float32)
            key_slab = lax.dynamic_slice_in_dim(key_heads, row_idx, window, 0)
            value_slab = lax.dynamic_slice_in_dim(values, row_idx, window, 0)
            mask_slab = lax.dynamic_slice_in_dim(inside_grid, row_idx, window, 0)
            logit_list = []
            for row_step in range(window):
                for col_step in range(window):
                    shifted = key_slab[row_step, col_step:col_step + grid_w].astype(jnp.float32)
                    logits = lax.optimization_barrier(jnp.sum(query_row * shifted, -1)) * score_scale
                    inside = mask_slab[row_step, col_step:col_step + grid_w][:, None] > 0.5
                    logit_list.append(jnp.where(inside, logits, -1e+30))
            logits = jnp.stack(logit_list)
            row_max = lax.optimization_barrier(jnp.max(logits, 0))
            exponent = jnp.exp(logits - row_max)
            attention = (exponent / lax.optimization_barrier(jnp.sum(exponent, 0))).astype(jnp.bfloat16)
            accumulated = jnp.zeros((grid_w, HEADS, head_dim), jnp.float32)
            for row_step in range(window):
                for col_step in range(window):
                    shifted = value_slab[row_step, col_step:col_step + grid_w].astype(jnp.float32)
                    share = attention[row_step * window + col_step][:, :, None].astype(jnp.float32)
                    accumulated = accumulated + share * shifted
            return accumulated.astype(jnp.bfloat16)
        attended = lax.map(one_row, jnp.arange(grid_h, dtype=jnp.int32)).reshape(grid_h * grid_w, D)
        stream = stream + jnp.dot(attended, out_weight[layer_idx], preferred_element_type=jnp.float32)
    return stream.astype(jnp.bfloat16).reshape(grid_h, grid_w, D)
```

```python
import functools

import jax
import jax.numpy as jnp
from jax import lax
from jax.experimental import pallas as pl
from jax.experimental.pallas import tpu as pltpu
from jax.sharding import PartitionSpec as P

HEADS = 16
RADIUS = 4
TOK_H = 32
PATCH = 8
BAND = 8

VMEM = pl.BlockSpec(memory_space=pltpu.VMEM)


def normed(stream, gain_row):
    centre = jnp.mean(stream, -1, keepdims=True)
    spread = jnp.mean(jnp.square(stream - centre), -1, keepdims=True)
    return ((stream - centre) * lax.rsqrt(spread + 1e-05) * gain_row).astype(jnp.bfloat16)


def regroup(token_cols, back=False):
    tokens = BAND * token_cols
    each = BAND * RADIUS
    shape = (tokens, tokens)
    grouped = lax.broadcasted_iota(jnp.int32, shape, 1 if back else 0)
    natural = lax.broadcasted_iota(jnp.int32, shape, 0 if back else 1)
    inner = grouped % each
    source = inner // RADIUS * token_cols + grouped // each * RADIUS + inner % RADIUS
    return (natural == source).astype(jnp.float32).astype(jnp.bfloat16)


def store_band(b, total, cells, stream, inputs):
    each = BAND * RADIUS
    units = each // inputs.shape[2]
    at = pl.ds(pl.multiple_of(b * each, each), each)
    for g in range(inputs.shape[0]):
        rows = slice(g * each, (g + 1) * each)
        stream[g, at, :] = total[rows]
        inputs[g, pl.ds(b * units, units)] = cells[rows].reshape(
            units, each // units, cells.shape[1]
        )


def iota(shape, dim):
    return lax.broadcasted_iota(jnp.int32, shape, dim)


def hot(mask):
    return mask.astype(jnp.float32).astype(jnp.bfloat16)


def rows_dot(a, b):
    return lax.dot_general(a, b, (((1,), (1,)), ((), ())), preferred_element_type=jnp.float32)


def exact_dot(a, b):
    return jnp.dot(a, b, precision=lax.Precision.HIGHEST, preferred_element_type=jnp.float32)


def target_of(j, z, n):
    if j == n - 1:
        return z
    low = jnp.where(n - 1 - j > z, n - 1 - j, n - 2 - j)
    high = jnp.where(z > j, j, j + 1)
    return jnp.where(2 * z < n, low, high)


def exchange_kernel(
    sizes, capacity, token_cols, parts,
    scans, dest, offsets, profile, profiles, embed, gain,
    stream, inputs, bias,
    placed, got, weighted, marks_out, marks_in, marks, carried, passed,
    counts_out, counts_in, total, image, turned, embed2,
    place_sem, got_sem, place_mark_sem, mark_sem, local_sem, pass_sem, carry_sem,
    count_out_sem, count_in_sem,
):
    n_row, n_col = sizes
    blocks = dest.shape[1]
    profile_count, strip, lanes = profiles.shape
    channels = scans.shape[0] // (blocks * strip)
    slots = strip * capacity
    group = max(1, 16 // capacity)
    chunk = channels * lanes // parts
    tile_rows = TOK_H * PATCH
    keys = n_col * slots
    z, col = lax.axis_index("row"), lax.axis_index("col")
    mesh_ids = pl.DeviceIdType.MESH
    f32, bf16 = jnp.float32, jnp.bfloat16

    barrier = pltpu.get_barrier_semaphore()
    for d in range(1, n_col):
        pl.semaphore_signal(
            barrier, inc=1, device_id=(z, lax.rem(col + d, n_col)), device_id_type=mesh_ids
        )
    for d in range(1, n_row):
        pl.semaphore_signal(
            barrier, inc=1, device_id=(lax.rem(z + d, n_row), col), device_id_type=mesh_ids
        )

    dest_row, off_row, prof_row = dest[...], offsets[...], profile[...]
    square = jnp.broadcast_to(dest_row.astype(f32), (blocks, blocks))
    earlier = (square.T == square) & (iota((blocks, blocks), 0) < iota((blocks, blocks), 1))
    rank_row = jnp.sum(earlier.astype(f32), 0, keepdims=True).astype(jnp.int32)

    tile_shape = (n_col * 8, blocks)
    step_row = iota(tile_shape, 0) % 8
    tile = jnp.where(step_row < n_row, step_row * n_col + iota(tile_shape, 0) // 8, -1)
    to_tile = hot(tile == dest_row)
    same = iota((128, blocks), 0) % capacity == rank_row
    for n, what in enumerate((off_row, prof_row)):
        value = jnp.where(same, what + 1, 0).astype(f32).astype(bf16)
        marks_out[:, n * 8 : (n + 1) * 8, :] = rows_dot(to_tile, value).reshape(n_col, 8, 128)

    own_profile = (
        iota((blocks, blocks), 0) == jnp.broadcast_to(prof_row, (blocks, blocks))
    ).astype(f32).T[:, :profile_count]
    for i in range(strip):
        weight = exact_dot(own_profile, profiles[:, i, :])
        for c in range(channels):
            block_row = scans[pl.ds(i * channels + c, blocks, stride=strip * channels), :]
            weighted[
                i // group,
                i % group * blocks : (i % group + 1) * blocks,
                c * lanes : (c + 1) * lanes,
            ] = (block_row * weight).astype(bf16)

    pl.semaphore_wait(barrier, n_col - 1 + n_row - 1)

    slot_row = jnp.concatenate(
        [dest_row * (group * capacity) + ig * capacity + rank_row for ig in range(group)], 1
    )
    per_step = n_col * group * capacity
    for d in range(1, n_col):
        peer = lax.rem(col + d, n_col)
        pltpu.make_async_remote_copy(
            src_ref=marks_out.at[peer],
            dst_ref=marks_in.at[col],
            send_sem=place_mark_sem,
            recv_sem=mark_sem,
            device_id=(z, peer),
            device_id_type=mesh_ids,
        ).start()
    for j in range(n_row):
        t = target_of(j, z, n_row)
        pick = hot(iota((per_step, group * blocks), 0) + t * per_step == slot_row)
        for h in range(parts):
            for g in range(strip // group):
                y = jnp.dot(
                    pick,
                    weighted[g, :, h * chunk : (h + 1) * chunk],
                    preferred_element_type=f32,
                ).astype(bf16)
                placed[t, h, :, g * group * capacity : (g + 1) * group * capacity, :] = y.reshape(
                    n_col, group * capacity, chunk
                )
            pltpu.make_async_copy(
                placed.at[t, h, col], got.at[t, h, col], local_sem.at[j, h]
            ).start()
            for d in range(1, n_col):
                peer = lax.rem(col + d, n_col)
                pltpu.make_async_remote_copy(
                    src_ref=placed.at[t, h, peer],
                    dst_ref=got.at[t, h, col],
                    send_sem=place_sem,
                    recv_sem=got_sem.at[j, h],
                    device_id=(z, peer),
                    device_id_type=mesh_ids,
                ).start()

    depth = embed.shape[0]
    pick_shape = (depth, depth)
    inner = depth // PATCH
    source = iota(pick_shape, 0) % inner * PATCH + iota(pick_shape, 0) // inner
    reorder = hot(iota(pick_shape, 1) == source)
    for n in range(0, embed.shape[1], 256):
        embed2[:, n : n + 256] = jnp.dot(
            reorder, embed[:, n : n + 256], preferred_element_type=f32
        ).astype(bf16)
    window_bias(token_cols, sizes, bias)

    pltpu.make_async_copy(
        marks_in.at[: n_col - 1], marks_in.at[: n_col - 1], mark_sem
    ).wait()
    per_tile = 128 // slots
    for u in range(keys // 128):
        mark = jnp.zeros((16, 128), f32)
        for s in range(per_tile):
            src = u * per_tile + s
            seen = jnp.where(src == col, marks_out[src], marks_in[src])
            mark = jnp.where(iota((16, 128), 1) // slots == s, seen, mark)
        marks[:, u * 128 : (u + 1) * 128] = mark
    strip_row = iota((1, keys), 1) % slots // capacity
    pixel = iota((tile_rows, keys), 0)
    for j in range(n_row):
        t = target_of(j, z, n_row)
        place = marks[pl.ds(t, 1), :].astype(jnp.int32)
        which = marks[pl.ds(t + 8, 1), :].astype(jnp.int32)
        row_of = jnp.where(place > 0, place - 1 + strip_row, -1)
        spread = hot(pixel == row_of)
        first = jnp.where(strip_row == 0, which, 0)
        by_profile = hot(iota((profile_count, keys), 0) + 1 == first)
        count = rows_dot(by_profile, spread).astype(bf16)
        last = j == n_row - 1
        if last:
            counts_in[z] = count
        else:
            counts_out[t] = count
            pltpu.make_async_remote_copy(
                src_ref=counts_out.at[t],
                dst_ref=counts_in.at[z],
                send_sem=count_out_sem,
                recv_sem=count_in_sem,
                device_id=(t, col),
                device_id_type=mesh_ids,
            ).start()
            up = t > z
            near = jnp.where(up, z + 1, z - 1)
            slot = jnp.where(jnp.logical_not(up) & (near == t), n_row, t)
            has = jnp.where(up, z > 0, z < n_row - 1)
        for h in range(parts):
            pltpu.make_async_copy(
                placed.at[t, h, col], got.at[t, h, col], local_sem.at[j, h]
            ).wait()
            pltpu.make_async_copy(
                got.at[t, h, : n_col - 1], got.at[t, h, : n_col - 1], got_sem.at[j, h]
            ).wait()
            part = jnp.dot(
                spread, got[t, h].reshape(keys, chunk), preferred_element_type=f32
            )
            if last:
                total[h] = part
                for there, here in ((z > 0, z), (z < n_row - 1, n_row)):

                    @pl.when(there)
                    def _(here=here, h=h):
                        pltpu.make_async_copy(
                            carried.at[here, h], carried.at[here, h], carry_sem.at[here, h]
                        ).wait()
                        total[h] += carried[here, h].astype(f32)
            else:

                @pl.when(has)
                def _(part=part, t=t, h=h):
                    pltpu.make_async_copy(
                        carried.at[t, h], carried.at[t, h], carry_sem.at[t, h]
                    ).wait()
                    passed[t, h] = (part + carried[t, h].astype(f32)).astype(bf16)

                @pl.when(jnp.logical_not(has))
                def _(part=part, t=t, h=h):
                    passed[t, h] = part.astype(bf16)

                pltpu.make_async_remote_copy(
                    src_ref=passed.at[t, h],
                    dst_ref=carried.at[slot, h],
                    send_sem=pass_sem,
                    recv_sem=carry_sem.at[slot, h],
                    device_id=(near, col),
                    device_id_type=mesh_ids,
                ).start()

    pltpu.make_async_copy(
        counts_in.at[: n_row - 1], counts_in.at[: n_row - 1], count_in_sem
    ).wait()
    count = counts_in[0].astype(f32)
    for s in range(1, n_row):
        count += counts_in[s].astype(f32)
    den = jnp.ones((tile_rows, lanes), f32)
    for i in range(strip):
        shifted = count if i == 0 else pltpu.roll(count, i, 1)
        den += exact_dot(shifted.T, profiles[:, i, :])
    per_part = chunk // lanes
    for c in range(channels):
        h, at = c // per_part, c % per_part * lanes
        image[c] = (total[h, :, at : at + lanes] / den).astype(bf16).astype(f32)

    def turn(i, carry):
        rows = pl.ds(pl.multiple_of(i * PATCH, PATCH), PATCH)
        block = image[:, rows, :].reshape(channels * PATCH, lanes)
        turned[pl.ds(pl.multiple_of(i * lanes, lanes), lanes), :] = block.T
        return carry

    lax.fori_loop(0, TOK_H, turn, 0, unroll=4)
    part_tokens = BAND * token_cols
    order = regroup(token_cols)

    def embed_part(k, carry):
        pieces = [
            turned[pl.ds(k * part_tokens * PATCH + q, part_tokens, stride=PATCH), :]
            for q in range(PATCH)
        ]
        lhs = jnp.concatenate(pieces, 1).astype(bf16)
        lhs = jnp.dot(order, lhs, preferred_element_type=f32).astype(bf16)
        out = jnp.dot(lhs, embed2[...], preferred_element_type=f32)
        store_band(k, out, normed(out, gain[0:1, :]), stream, inputs)
        return carry

    lax.fori_loop(0, TOK_H // BAND, embed_part, 0)

    for src, sem in (
        (marks_out.at[: n_col - 1], place_mark_sem),
        (placed.at[:, :, : n_col - 1], place_sem),
        (counts_out.at[: n_row - 1], count_out_sem),
        (passed.at[: n_row - 1], pass_sem),
    ):
        pltpu.make_async_copy(src, src, sem).wait()


def layer_kernel(layer, last, token_cols, sizes, x, qkv, out_w, stream, bias, gain, *refs):
    outs, refs = (refs[:1], refs[1:]) if last else (refs[:2], refs[2:])
    q_ref, kv, w, wo, xh, w_sem, send, recv = refs
    width = wo.shape[0]
    head_dim = width // HEADS
    groups, units, unit, _ = x.shape
    own = units * unit
    count = groups * own
    loads = [
        pltpu.make_async_copy(
            qkv.at[layer, :, n * width : (n + 1) * width], w.at[n], w_sem.at[n]
        )
        for n in range(3)
    ] + [pltpu.make_async_copy(out_w.at[layer], wo, w_sem.at[3])]
    for load in loads:
        load.start()

    row, col = lax.axis_index("row"), lax.axis_index("col")
    up, down = row > 0, row < sizes[0] - 1
    west, east = col > 0, col < sizes[1] - 1
    top, bottom = xh.at[:groups], xh.at[groups : 2 * groups]
    l0 = 2 * groups
    r0 = l0 + units + 2
    end = r0 + units + 2
    moves = [
        (-1, 0, up, x.at[:, 0], bottom, top),
        (1, 0, down, x.at[:, units - 1], top, bottom),
        (0, -1, west, x.at[0], xh.at[r0 + 1 : end - 1], xh.at[l0 + 1 : r0 - 1]),
        (0, 1, east, x.at[groups - 1], xh.at[l0 + 1 : r0 - 1], xh.at[r0 + 1 : end - 1]),
        (-1, -1, up & west, x.at[0, 0], xh.at[end - 1], xh.at[l0]),
        (-1, 1, up & east, x.at[groups - 1, 0], xh.at[r0 - 1], xh.at[r0]),
        (1, -1, down & west, x.at[0, units - 1], xh.at[r0], xh.at[r0 - 1]),
        (1, 1, down & east, x.at[groups - 1, units - 1], xh.at[l0], xh.at[end - 1]),
    ]
    opposite = [1, 0, 3, 2, 7, 6, 5, 4]
    barrier = pltpu.get_barrier_semaphore()
    mesh_ids = pl.DeviceIdType.MESH
    for dr, dc, there, _, _, _ in moves:

        @pl.when(there)
        def _(dr=dr, dc=dc):
            pl.semaphore_signal(
                barrier, inc=1, device_id=(row + dr, col + dc), device_id_type=mesh_ids
            )

    for _, _, there, _, _, here in moves:

        @pl.when(jnp.logical_not(there))
        def _(here=here):
            here[...] = jnp.zeros(here.shape, here.dtype)

    rows_near = 1 + up.astype(jnp.int32) + down.astype(jnp.int32)
    cols_near = 1 + west.astype(jnp.int32) + east.astype(jnp.int32)
    pl.semaphore_wait(barrier, rows_near * cols_near - 1)
    copies = []
    for n, (dr, dc, there, source, lands, _) in enumerate(moves):
        copies.append(
            pltpu.make_async_remote_copy(
                src_ref=source,
                dst_ref=lands,
                send_sem=send.at[n],
                recv_sem=recv.at[n],
                device_id=(row + dr, col + dc),
                device_id_type=mesh_ids,
            )
        )

        @pl.when(there)
        def _(copy=copies[-1]):
            copy.start()

    step = 512

    def project(n, put):
        rows = x if n < 3 else xh
        weight = w.at[n] if n < 3 else w.at[n - 2]
        total = count if n < 3 else end * unit

        def part(k, c):
            cols = pl.ds(pl.multiple_of(k * step, step), step)
            y = jnp.dot(
                rows[...].reshape(total, width),
                weight[:, cols],
                preferred_element_type=jnp.float32,
            ).astype(jnp.bfloat16)
            put(k, y)
            return c

        lax.fori_loop(0, width // step, part, 0)

    def put_q(k, y):
        cols = pl.ds(pl.multiple_of(k * step, step), step)
        for g in range(groups):
            q_ref[g, :, cols] = (y[g * own : (g + 1) * own] * head_dim ** (-0.5)).astype(
                jnp.bfloat16
            )

    def put_own(base, k, y):
        cols = pl.ds(pl.multiple_of(base + k * step, step), step)
        for g in range(groups):
            kv[g + 1, unit : unit + own, cols] = y[g * own : (g + 1) * own]

    def put_halo(base, k, y):
        cols = pl.ds(pl.multiple_of(base + k * step, step), step)
        for g in range(groups):
            kv[g + 1, :unit, cols] = y[g * unit : (g + 1) * unit]
            kv[g + 1, unit + own :, cols] = y[(groups + g) * unit : (groups + g + 1) * unit]
        kv[0, :, cols] = y[l0 * unit : r0 * unit]
        kv[groups + 1, :, cols] = y[r0 * unit :]

    loads[0].wait()
    project(0, put_q)
    for n in (1, 2):
        loads[n].wait()
        project(n, functools.partial(put_own, (n - 1) * width))
    for n, (_, _, there, _, _, here) in enumerate(moves):

        @pl.when(there)
        def _(n=n, here=here):
            copies[n].wait_send()
            pltpu.make_async_remote_copy(
                src_ref=here,
                dst_ref=here,
                send_sem=send.at[n],
                recv_sem=recv.at[opposite[n]],
                device_id=(row + moves[n][0], col + moves[n][1]),
                device_id_type=mesh_ids,
            ).wait_recv()

    for n in (3, 4):
        project(n, functools.partial(put_halo, (n - 3) * width))
    loads[3].wait()
    each = BAND * RADIUS
    span = (BAND + 2 * RADIUS) * RADIUS
    pair = 2 * head_dim
    queries = 2 * each
    low = lax.broadcasted_iota(jnp.int32, (queries, pair), 1) < head_dim
    ones = jnp.ones((4 * span, pair), jnp.bfloat16)
    order = regroup(token_cols, True) if last else None

    def band(b, carry):
        q_at = pl.ds(pl.multiple_of(b * each, each), each)
        k_at = pl.ds(pl.multiple_of(b * each, each), span)
        halves = []
        for s in range(groups // 2):
            half_bias = bias[b, s]
            both = jnp.concatenate([half_bias, half_bias], 0)
            pieces = []
            for h in range(HEADS // 2):
                cols = slice(h * pair, (h + 1) * pair)
                v_cols = slice(width + h * pair, width + (h + 1) * pair)
                q = jnp.concatenate([q_ref[2 * s + i, q_at, cols] for i in range(2)], 0)
                zero = jnp.zeros_like(q)
                q2 = jnp.concatenate([jnp.where(low, q, zero), jnp.where(low, zero, q)], 0)
                k = jnp.concatenate([kv[2 * s + i, k_at, cols] for i in range(4)], 0)
                v = jnp.concatenate([kv[2 * s + i, k_at, v_cols] for i in range(4)], 0)
                logits = lax.dot_general(
                    q2, k, (((1,), (1,)), ((), ())), preferred_element_type=jnp.float32
                )
                logits = logits + both
                top_logit = jnp.max(logits, -1, keepdims=True)
                weight = jnp.exp(logits - top_logit).astype(jnp.bfloat16)
                summed = jnp.dot(
                    weight, jnp.concatenate([v, ones], 1), preferred_element_type=jnp.float32
                )
                share = summed[:, :pair] / summed[:, pair:]
                pieces.append(
                    jnp.where(low, share[:queries], share[queries:]).astype(jnp.bfloat16)
                )
            halves.append(jnp.concatenate(pieces, 1))
        attended = jnp.concatenate(halves, 0)
        before = jnp.concatenate([stream[g, q_at, :] for g in range(groups)], 0)
        total = before + jnp.dot(attended, wo[...], preferred_element_type=jnp.float32)
        if last:
            rows = BAND * token_cols
            outs[0][pl.ds(pl.multiple_of(b * rows, rows), rows), :] = jnp.dot(
                order, total.astype(jnp.bfloat16), preferred_element_type=jnp.float32
            ).astype(jnp.bfloat16)
        else:
            store_band(b, total, normed(total, gain[...]), outs[0], outs[1])
        return carry

    lax.fori_loop(0, TOK_H // BAND, band, 0)


def window_bias(token_cols, sizes, bias):
    win = BAND + 2 * RADIUS
    shape = bias.shape[2:]
    q, k = iota(shape, 0), iota(shape, 1)
    q_row = q % (BAND * RADIUS) // RADIUS
    q_col = q // (BAND * RADIUS) * RADIUS + q % RADIUS
    k_row = k % (win * RADIUS) // RADIUS - RADIUS
    k_col = k // (win * RADIUS) * RADIUS + k % RADIUS - RADIUS
    near = (jnp.abs(k_row - q_row) <= RADIUS) & (jnp.abs(k_col - q_col) <= RADIUS)
    for b in range(bias.shape[0]):
        g_row = lax.axis_index("row") * TOK_H + b * BAND + k_row
        row_in = near & (g_row >= 0) & (g_row < TOK_H * sizes[0])
        for s in range(bias.shape[1]):
            g_col = lax.axis_index("col") * token_cols + s * 2 * RADIUS + k_col
            inside = row_in & (g_col >= 0) & (g_col < token_cols * sizes[1])
            bias[b, s] = jnp.where(inside, 0.0, -1e30)


def per_device(
    scans, dest, offsets, profile_index, profiles, embed_weight, attn_gain, qkv_weight, out_weight
):
    sizes = (lax.axis_size("row"), lax.axis_size("col"))
    n_row, n_col = sizes
    blocks, strip, channels, tile_cols = scans.shape
    token_cols = tile_cols // PATCH
    count = TOK_H * token_cols
    tile_rows = TOK_H * PATCH
    profile_count = profiles.shape[0]
    depth, width = embed_weight.shape
    layers = qkv_weight.shape[0]
    capacity = max(2, 2 * blocks // (n_row * n_col))
    capacity = -(-capacity * strip // 16) * 16 // strip
    slots = strip * capacity
    group = max(1, 16 // capacity)
    parts = 2
    chunk = channels * tile_cols // parts
    f32, bf16 = jnp.float32, jnp.bfloat16

    groups = token_cols // RADIUS
    unit = RADIUS * RADIUS
    units = TOK_H // RADIUS
    state = (
        jax.ShapeDtypeStruct((groups, units * unit, width), f32),
        jax.ShapeDtypeStruct((groups, units, unit, width), bf16),
    )
    win = BAND + 2 * RADIUS
    masks = (TOK_H // BAND, token_cols // (2 * RADIUS), 2 * BAND * RADIUS, 4 * win * RADIUS)
    dma = pltpu.SemaphoreType.DMA
    stream, inputs, bias = pl.pallas_call(
        functools.partial(exchange_kernel, sizes, capacity, token_cols, parts),
        out_shape=state + (jax.ShapeDtypeStruct(masks, f32),),
        in_specs=[VMEM] * 7,
        out_specs=(VMEM,) * 3,
        scratch_shapes=[
            pltpu.VMEM((n_row, parts, n_col, slots, chunk), bf16),
            pltpu.VMEM((n_row, parts, n_col, slots, chunk), bf16),
            pltpu.VMEM((strip // group, group * blocks, channels * tile_cols), bf16),
            pltpu.VMEM((n_col, 16, 128), f32),
            pltpu.VMEM((n_col, 16, 128), f32),
            pltpu.VMEM((16, n_col * slots), f32),
            pltpu.VMEM((n_row + 1, parts, tile_rows, chunk), bf16),
            pltpu.VMEM((n_row, parts, tile_rows, chunk), bf16),
            pltpu.VMEM((n_row, profile_count, tile_rows), bf16),
            pltpu.VMEM((n_row, profile_count, tile_rows), bf16),
            pltpu.VMEM((parts, tile_rows, chunk), f32),
            pltpu.VMEM((channels, tile_rows, tile_cols), f32),
            pltpu.VMEM((TOK_H * tile_cols, PATCH * channels), f32),
            pltpu.VMEM((depth, width), bf16),
            dma,
            dma((n_row, parts)),
            dma,
            dma,
            dma((n_row, parts)),
            dma,
            dma((n_row + 1, parts)),
            dma,
            dma,
        ],
        compiler_params=pltpu.CompilerParams(
            vmem_limit_bytes=56 * 2**20, collective_id=layers, has_side_effects=True
        ),
        name="exchange",
    )(
        scans.reshape(blocks * strip * channels, tile_cols),
        dest.reshape(1, blocks),
        offsets.reshape(1, blocks),
        profile_index.reshape(1, blocks),
        profiles,
        embed_weight,
        attn_gain,
    )
    hbm = pl.BlockSpec(memory_space=pl.ANY)
    for l in range(layers):
        last = l == layers - 1
        result = pl.pallas_call(
            functools.partial(layer_kernel, l, last, token_cols, sizes),
            out_shape=jax.ShapeDtypeStruct((count, width), bf16) if last else state,
            in_specs=[VMEM, hbm, hbm, VMEM, VMEM, VMEM],
            out_specs=VMEM if last else (VMEM,) * 2,
            scratch_shapes=[
                pltpu.VMEM((groups, units * unit, width), bf16),
                pltpu.VMEM((groups + 2, (units + 2) * unit, 2 * width), bf16),
                pltpu.VMEM((3, width, width), bf16),
                pltpu.VMEM((width, width), bf16),
                pltpu.VMEM((2 * groups + 2 * (units + 2), unit, width), bf16),
                pltpu.SemaphoreType.DMA((4,)),
                pltpu.SemaphoreType.DMA((8,)),
                pltpu.SemaphoreType.DMA((8,)),
            ],
            compiler_params=pltpu.CompilerParams(
                vmem_limit_bytes=56 * 2**20, collective_id=l, has_side_effects=True
            ),
            name="layer" + str(l),
        )(
            inputs,
            qkv_weight,
            out_weight,
            stream,
            bias,
            attn_gain[min(l + 1, layers - 1)][None],
        )
        if last:
            return result.reshape(TOK_H, token_cols, width)
        stream, inputs = result


def solution(mesh):
    placed = (
        P(("row", "col"), None, None, None),
        P(("row", "col"), None),
        P(("row", "col")),
        P(("row", "col")),
        P(),
        P(),
        P(),
        P(),
        P(),
    )
    return jax.shard_map(
        per_device, mesh=mesh, in_specs=placed, out_specs=P("row", "col", None), check_vma=False
    )
```

```python
import functools

import jax
import jax.numpy as jnp
from jax import lax
from jax.experimental import pallas as pl
from jax.experimental.pallas import tpu as pltpu
from jax.sharding import PartitionSpec as P

HEADS = 16
RADIUS = 4
TOK_H = 32
PATCH = 8
BAND = 8

VMEM = pl.BlockSpec(memory_space=pltpu.VMEM)


def normed(stream, gain_row):
    centre = jnp.mean(stream, -1, keepdims=True)
    spread = jnp.mean(jnp.square(stream - centre), -1, keepdims=True)
    return ((stream - centre) * lax.rsqrt(spread + 1e-05) * gain_row).astype(jnp.bfloat16)


def regroup(token_cols, back=False):
    tokens = BAND * token_cols
    each = BAND * RADIUS
    shape = (tokens, tokens)
    grouped = lax.broadcasted_iota(jnp.int32, shape, 1 if back else 0)
    natural = lax.broadcasted_iota(jnp.int32, shape, 0 if back else 1)
    inner = grouped % each
    source = inner // RADIUS * token_cols + grouped // each * RADIUS + inner % RADIUS
    return (natural == source).astype(jnp.float32).astype(jnp.bfloat16)


def store_band(b, total, stream):
    each = BAND * RADIUS
    at = pl.ds(pl.multiple_of(b * each, each), each)
    for g in range(stream.shape[0]):
        stream[g, at, :] = total[g * each : (g + 1) * each]


def load_band(b, stream):
    each = BAND * RADIUS
    at = pl.ds(pl.multiple_of(b * each, each), each)
    return jnp.concatenate([stream[g, at, :] for g in range(stream.shape[0])], 0)


def store_cells(b, cells, inputs):
    each = BAND * RADIUS
    units = each // inputs.shape[2]
    for g in range(inputs.shape[0]):
        rows = slice(g * each, (g + 1) * each)
        inputs[g, pl.ds(b * units, units)] = cells[rows].reshape(
            units, each // units, cells.shape[1]
        )


def iota(shape, dim):
    return lax.broadcasted_iota(jnp.int32, shape, dim)


def hot(mask):
    return mask.astype(jnp.float32).astype(jnp.bfloat16)


def rows_dot(a, b):
    return lax.dot_general(a, b, (((1,), (1,)), ((), ())), preferred_element_type=jnp.float32)


def exact_dot(a, b):
    return jnp.dot(a, b, precision=lax.Precision.HIGHEST, preferred_element_type=jnp.float32)


def target_of(j, z, n):
    if j == n - 1:
        return z
    low = jnp.where(n - 1 - j > z, n - 1 - j, n - 2 - j)
    high = jnp.where(z > j, j, j + 1)
    return jnp.where(2 * z < n, low, high)


def window_bias(token_cols, sizes, bias):
    win = BAND + 2 * RADIUS
    shape = bias.shape[2:]
    q, k = iota(shape, 0), iota(shape, 1)
    q_row = q % (BAND * RADIUS) // RADIUS
    q_col = q // (BAND * RADIUS) * RADIUS + q % RADIUS
    k_row = k % (win * RADIUS) // RADIUS - RADIUS
    k_col = k // (win * RADIUS) * RADIUS + k % RADIUS - RADIUS
    near = (jnp.abs(k_row - q_row) <= RADIUS) & (jnp.abs(k_col - q_col) <= RADIUS)
    for b in range(bias.shape[0]):
        g_row = lax.axis_index("row") * TOK_H + b * BAND + k_row
        row_in = near & (g_row >= 0) & (g_row < TOK_H * sizes[0])
        for s in range(bias.shape[1]):
            g_col = lax.axis_index("col") * token_cols + s * 2 * RADIUS + k_col
            inside = row_in & (g_col >= 0) & (g_col < token_cols * sizes[1])
            bias[b, s] = jnp.where(inside, 0.0, -1e30)


def whole_kernel(
    sizes, capacity, token_cols, parts,
    scans_hbm, dest, offsets, profile, profiles, embed_hbm, gain, qkv, out_w,
    out,
    scans, embed, placed, got, weighted, marks_out, marks_in, marks, carried, passed,
    counts_out, counts_in, total, den, image, turned, embed2, stream, xs, xhs, bias, q_ref, kv, w, wo,
    load_sem, w_sem, place_sem, got_sem, place_mark_sem, mark_sem, local_sem, pass_sem,
    carry_sem, count_out_sem, count_in_sem, send, recv,
):
    n_row, n_col = sizes
    layers = w.shape[0]
    blocks = dest.shape[1]
    profile_count, strip, lanes = profiles.shape
    channels = scans.shape[0] // (blocks * strip)
    slots = strip * capacity
    group = max(1, 16 // capacity)
    chunk = channels * lanes // parts
    tile_rows = TOK_H * PATCH
    keys = n_col * slots
    bands = TOK_H // BAND
    z, col = lax.axis_index("row"), lax.axis_index("col")
    mesh_ids = pl.DeviceIdType.MESH
    f32, bf16 = jnp.float32, jnp.bfloat16
    width = wo.shape[2]
    head_dim = width // HEADS
    groups, units, unit = xs.shape[1:4]
    own = units * unit
    count = groups * own

    loads = [
        pltpu.make_async_copy(scans_hbm, scans, load_sem.at[0]),
        pltpu.make_async_copy(embed_hbm, embed, load_sem.at[1]),
    ]
    w_loads = [
        [
            pltpu.make_async_copy(
                qkv.at[l, :, n * width : (n + 1) * width], w.at[l, n], w_sem.at[l, n]
            )
            for n in range(3)
        ]
        + [pltpu.make_async_copy(out_w.at[l], wo.at[l], w_sem.at[l, 3])]
        for l in range(layers)
    ]
    for load in loads:
        load.start()

    up, down = z > 0, z < n_row - 1
    west, east = col > 0, col < n_col - 1
    l0 = 2 * groups
    r0 = l0 + units + 2
    end = r0 + units + 2
    where = [
        (-1, 0, up), (1, 0, down), (0, -1, west), (0, 1, east),
        (-1, -1, up & west), (-1, 1, up & east), (1, -1, down & west), (1, 1, down & east),
    ]
    opposite = [1, 0, 3, 2, 7, 6, 5, 4]

    def pieces(l):
        x, xh = xs.at[l], xhs.at[l]
        top, bottom = xh.at[:groups], xh.at[groups : 2 * groups]
        left, right = xh.at[l0 + 1 : r0 - 1], xh.at[r0 + 1 : end - 1]
        return [
            (x.at[:, 0], bottom, top),
            (x.at[:, units - 1], top, bottom),
            (x.at[0], right, left),
            (x.at[groups - 1], left, right),
            (x.at[0, 0], xh.at[end - 1], xh.at[l0]),
            (x.at[groups - 1, 0], xh.at[r0 - 1], xh.at[r0]),
            (x.at[0, units - 1], xh.at[r0], xh.at[r0 - 1]),
            (x.at[groups - 1, units - 1], xh.at[l0], xh.at[end - 1]),
        ]

    def send_halo(l, n, at=None):
        dr, dc, there = where[n]
        source, lands, _ = pieces(l)[n]
        if at is not None:
            source, lands = source.at[at], lands.at[at]

        @pl.when(there)
        def _():
            pltpu.make_async_remote_copy(
                src_ref=source,
                dst_ref=lands,
                send_sem=send.at[l, n],
                recv_sem=recv.at[l, n],
                device_id=(z + dr, col + dc),
                device_id_type=mesh_ids,
            ).start()

    def send_band(l, b):
        per_band = BAND // RADIUS
        at = pl.ds(b * per_band, per_band)
        send_halo(l, 2, at)
        send_halo(l, 3, at)

        @pl.when(b == 0)
        def _():
            for n in (0, 4, 5):
                send_halo(l, n)

        @pl.when(b == bands - 1)
        def _():
            for n in (1, 6, 7):
                send_halo(l, n)

    def wait_halo(l):
        for n, (_, _, there) in enumerate(where):
            source, _, here = pieces(l)[n]

            @pl.when(there)
            def _(n=n, source=source, here=here):
                pltpu.make_async_copy(source, source, send.at[l, n]).wait()
                pltpu.make_async_copy(here, here, recv.at[l, opposite[n]]).wait()

    barrier = pltpu.get_barrier_semaphore()
    for d in range(1, n_col):
        pl.semaphore_signal(
            barrier, inc=1, device_id=(z, lax.rem(col + d, n_col)), device_id_type=mesh_ids
        )
    for d in range(1, n_row):
        pl.semaphore_signal(
            barrier, inc=1, device_id=(lax.rem(z + d, n_row), col), device_id_type=mesh_ids
        )
    for dr, dc, there in where[4:]:

        @pl.when(there)
        def _(dr=dr, dc=dc):
            pl.semaphore_signal(
                barrier, inc=1, device_id=(z + dr, col + dc), device_id_type=mesh_ids
            )

    for l in range(layers):
        for n, (_, _, there) in enumerate(where):
            here = pieces(l)[n][2]

            @pl.when(jnp.logical_not(there))
            def _(here=here):
                here[...] = jnp.zeros(here.shape, here.dtype)

    dest_row, off_row, prof_row = dest[...], offsets[...], profile[...]
    square = jnp.broadcast_to(dest_row.astype(f32), (blocks, blocks))
    earlier = (square.T == square) & (iota((blocks, blocks), 0) < iota((blocks, blocks), 1))
    rank_row = jnp.sum(earlier.astype(f32), 0, keepdims=True).astype(jnp.int32)

    tile_shape = (n_col * 8, blocks)
    step_row = iota(tile_shape, 0) % 8
    tile = jnp.where(step_row < n_row, step_row * n_col + iota(tile_shape, 0) // 8, -1)
    to_tile = hot(tile == dest_row)
    same = iota((128, blocks), 0) % capacity == rank_row
    for n, what in enumerate((off_row, prof_row)):
        value = jnp.where(same, what + 1, 0).astype(f32).astype(bf16)
        marks_out[:, n * 8 : (n + 1) * 8, :] = rows_dot(to_tile, value).reshape(n_col, 8, 128)

    own_profile = (
        iota((blocks, blocks), 0) == jnp.broadcast_to(prof_row, (blocks, blocks))
    ).astype(f32).T[:, :profile_count]
    loads[0].wait()
    for i in range(strip):
        weight = exact_dot(own_profile, profiles[:, i, :])
        for c in range(channels):
            block_row = scans[pl.ds(i * channels + c, blocks, stride=strip * channels), :]
            weighted[
                i // group,
                i % group * blocks : (i % group + 1) * blocks,
                c * lanes : (c + 1) * lanes,
            ] = (block_row * weight).astype(bf16)

    for load in sum(w_loads, []):
        load.start()
    rows_near = up.astype(jnp.int32) + down.astype(jnp.int32)
    cols_near = west.astype(jnp.int32) + east.astype(jnp.int32)
    pl.semaphore_wait(barrier, n_col - 1 + n_row - 1 + rows_near * cols_near)

    slot_row = jnp.concatenate(
        [dest_row * (group * capacity) + ig * capacity + rank_row for ig in range(group)], 1
    )
    per_step = n_col * group * capacity
    for d in range(1, n_col):
        peer = lax.rem(col + d, n_col)
        pltpu.make_async_remote_copy(
            src_ref=marks_out.at[peer],
            dst_ref=marks_in.at[col],
            send_sem=place_mark_sem,
            recv_sem=mark_sem,
            device_id=(z, peer),
            device_id_type=mesh_ids,
        ).start()
    for j in range(n_row):
        t = target_of(j, z, n_row)
        pick = hot(iota((per_step, group * blocks), 0) + t * per_step == slot_row)
        for h in range(parts):
            for g in range(strip // group):
                y = jnp.dot(
                    pick,
                    weighted[g, :, h * chunk : (h + 1) * chunk],
                    preferred_element_type=f32,
                ).astype(bf16)
                placed[t, h, :, g * group * capacity : (g + 1) * group * capacity, :] = y.reshape(
                    n_col, group * capacity, chunk
                )
            pltpu.make_async_copy(
                placed.at[t, h, col], got.at[t, h, col], local_sem.at[j, h]
            ).start()
            for d in range(1, n_col):
                peer = lax.rem(col + d, n_col)
                pltpu.make_async_remote_copy(
                    src_ref=placed.at[t, h, peer],
                    dst_ref=got.at[t, h, col],
                    send_sem=place_sem,
                    recv_sem=got_sem.at[j, h],
                    device_id=(z, peer),
                    device_id_type=mesh_ids,
                ).start()

    def prepare():
        loads[1].wait()
        depth = embed.shape[0] // parts
        pick_shape = (depth, depth)
        inner = depth // PATCH
        source = iota(pick_shape, 0) % inner * PATCH + iota(pick_shape, 0) // inner
        reorder = hot(iota(pick_shape, 1) == source)
        for h in range(parts):
            for n in range(0, embed.shape[1], 512):
                embed2[h, :, n : n + 512] = jnp.dot(
                    reorder,
                    embed[h * depth : (h + 1) * depth, n : n + 512],
                    preferred_element_type=f32,
                ).astype(bf16)
        window_bias(token_cols, sizes, bias)

    def denominator():
        pltpu.make_async_copy(
            counts_in.at[: n_row - 1], counts_in.at[: n_row - 1], count_in_sem
        ).wait()
        hits = counts_in[0].astype(f32)
        for s in range(1, n_row):
            hits += counts_in[s].astype(f32)
        divisor = jnp.ones((tile_rows, lanes), f32)
        for i in range(strip):
            shifted = hits if i == 0 else pltpu.roll(hits, i, 1)
            divisor += exact_dot(shifted.T, profiles[:, i, :])
        den[...] = divisor

    part_tokens = BAND * token_cols
    per_part = chunk // lanes
    order = regroup(token_cols)
    half_depth = embed_hbm.shape[0] // parts

    def embed_half(h):
        for c in range(per_part):
            pixels = total[h, :, c * lanes : (c + 1) * lanes] / den[...]
            image[c] = pixels.astype(bf16).astype(f32)

        def turn(i, carry):
            rows = pl.ds(pl.multiple_of(i * PATCH, PATCH), PATCH)
            block = image[:, rows, :].reshape(per_part * PATCH, lanes)
            turned[pl.ds(pl.multiple_of(i * lanes, lanes), lanes), :] = block.T
            return carry

        lax.fori_loop(0, TOK_H, turn, 0, unroll=8)

        def embed_part(n, carry):
            k = n if h < parts - 1 else jnp.where(n == 0, 0, jnp.where(n == 1, bands - 1, n - 1))
            lhs = jnp.concatenate(
                [
                    turned[pl.ds(k * part_tokens * PATCH + q, part_tokens, stride=PATCH), :]
                    for q in range(PATCH)
                ],
                1,
            ).astype(bf16)
            lhs = jnp.dot(order, lhs, preferred_element_type=f32).astype(bf16)
            part = jnp.dot(lhs, embed2[h], preferred_element_type=f32)
            if h > 0:
                part += load_band(k, stream)
            store_band(k, part, stream)
            if h == parts - 1:
                store_cells(k, normed(part, gain[0:1, :]), xs.at[0])
                send_band(0, k)
            return carry

        lax.fori_loop(0, bands, embed_part, 0)

    pltpu.make_async_copy(
        marks_in.at[: n_col - 1], marks_in.at[: n_col - 1], mark_sem
    ).wait()
    per_tile = 128 // slots
    for u in range(keys // 128):
        mark = jnp.zeros((16, 128), f32)
        for s in range(per_tile):
            src = u * per_tile + s
            seen = jnp.where(src == col, marks_out[src], marks_in[src])
            mark = jnp.where(iota((16, 128), 1) // slots == s, seen, mark)
        marks[:, u * 128 : (u + 1) * 128] = mark
    strip_row = iota((1, keys), 1) % slots // capacity
    pixel = iota((tile_rows, keys), 0)
    for j in range(n_row):
        t = target_of(j, z, n_row)
        place = marks[pl.ds(t, 1), :].astype(jnp.int32)
        which = marks[pl.ds(t + 8, 1), :].astype(jnp.int32)
        row_of = jnp.where(place > 0, place - 1 + strip_row, -1)
        spread = hot(pixel == row_of)
        first = jnp.where(strip_row == 0, which, 0)
        by_profile = hot(iota((profile_count, keys), 0) + 1 == first)
        count = rows_dot(by_profile, spread).astype(bf16)
        last = j == n_row - 1
        if j == min(1, n_row - 1):
            prepare()
        if last:
            counts_in[z] = count
        else:
            counts_out[t] = count
            pltpu.make_async_remote_copy(
                src_ref=counts_out.at[t],
                dst_ref=counts_in.at[z],
                send_sem=count_out_sem,
                recv_sem=count_in_sem,
                device_id=(t, col),
                device_id_type=mesh_ids,
            ).start()
            up = t > z
            near = jnp.where(up, z + 1, z - 1)
            slot = jnp.where(jnp.logical_not(up) & (near == t), n_row, t)
            has = jnp.where(up, z > 0, z < n_row - 1)
        for h in range(parts):
            pltpu.make_async_copy(
                placed.at[t, h, col], got.at[t, h, col], local_sem.at[j, h]
            ).wait()
            pltpu.make_async_copy(
                got.at[t, h, : n_col - 1], got.at[t, h, : n_col - 1], got_sem.at[j, h]
            ).wait()
            part = jnp.dot(
                spread, got[t, h].reshape(keys, chunk), preferred_element_type=f32
            )
            if last:
                if h == 0:
                    denominator()
                total[h] = part
                for there, here in ((z > 0, z), (z < n_row - 1, n_row)):

                    @pl.when(there)
                    def _(here=here, h=h):
                        pltpu.make_async_copy(
                            carried.at[here, h], carried.at[here, h], carry_sem.at[here, h]
                        ).wait()
                        total[h] += carried[here, h].astype(f32)

                embed_half(h)
            else:

                @pl.when(has)
                def _(part=part, t=t, h=h):
                    pltpu.make_async_copy(
                        carried.at[t, h], carried.at[t, h], carry_sem.at[t, h]
                    ).wait()
                    passed[t, h] = (part + carried[t, h].astype(f32)).astype(bf16)

                @pl.when(jnp.logical_not(has))
                def _(part=part, t=t, h=h):
                    passed[t, h] = part.astype(bf16)

                pltpu.make_async_remote_copy(
                    src_ref=passed.at[t, h],
                    dst_ref=carried.at[slot, h],
                    send_sem=pass_sem,
                    recv_sem=carry_sem.at[slot, h],
                    device_id=(near, col),
                    device_id_type=mesh_ids,
                ).start()


    step = 512

    def project(rows, weight, put):
        def part(k, c):
            cols = pl.ds(pl.multiple_of(k * step, step), step)
            y = jnp.dot(
                rows[...].reshape(-1, width), weight[:, cols], preferred_element_type=f32
            ).astype(bf16)
            put(k, y)
            return c

        lax.fori_loop(0, width // step, part, 0)

    def put_q(k, y):
        cols = pl.ds(pl.multiple_of(k * step, step), step)
        for g in range(groups):
            q_ref[g, :, cols] = (y[g * own : (g + 1) * own] * head_dim ** (-0.5)).astype(
                jnp.bfloat16
            )

    def put_own(base, k, y):
        cols = pl.ds(pl.multiple_of(base + k * step, step), step)
        for g in range(groups):
            kv[g + 1, unit : unit + own, cols] = y[g * own : (g + 1) * own]

    def put_halo(base, k, y):
        cols = pl.ds(pl.multiple_of(base + k * step, step), step)
        for g in range(groups):
            kv[g + 1, :unit, cols] = y[g * unit : (g + 1) * unit]
            kv[g + 1, unit + own :, cols] = y[(groups + g) * unit : (groups + g + 1) * unit]
        kv[0, :, cols] = y[l0 * unit : r0 * unit]
        kv[groups + 1, :, cols] = y[r0 * unit :]

    each = BAND * RADIUS
    span = (BAND + 2 * RADIUS) * RADIUS
    pair = 2 * head_dim
    queries = 2 * each
    low = lax.broadcasted_iota(jnp.int32, (queries, pair), 1) < head_dim
    ones = jnp.ones((4 * span, pair), jnp.bfloat16)
    back = regroup(token_cols, True)

    def band(l, n, carry):
        last = l == layers - 1
        b = n if last else jnp.where(n == 0, 0, jnp.where(n == 1, bands - 1, n - 1))
        q_at = pl.ds(pl.multiple_of(b * each, each), each)
        k_at = pl.ds(pl.multiple_of(b * each, each), span)
        halves = []
        for s in range(groups // 2):
            half_bias = bias[b, s]
            both = jnp.concatenate([half_bias, half_bias], 0)
            pieces = []
            for h in range(HEADS // 2):
                cols = slice(h * pair, (h + 1) * pair)
                v_cols = slice(width + h * pair, width + (h + 1) * pair)
                q = jnp.concatenate([q_ref[2 * s + i, q_at, cols] for i in range(2)], 0)
                zero = jnp.zeros_like(q)
                q2 = jnp.concatenate([jnp.where(low, q, zero), jnp.where(low, zero, q)], 0)
                k = jnp.concatenate([kv[2 * s + i, k_at, cols] for i in range(4)], 0)
                v = jnp.concatenate([kv[2 * s + i, k_at, v_cols] for i in range(4)], 0)
                logits = lax.dot_general(
                    q2, k, (((1,), (1,)), ((), ())), preferred_element_type=jnp.float32
                )
                logits = logits + both
                top_logit = jnp.max(logits, -1, keepdims=True)
                weight = jnp.exp(logits - top_logit).astype(jnp.bfloat16)
                summed = jnp.dot(
                    weight, jnp.concatenate([v, ones], 1), preferred_element_type=jnp.float32
                )
                share = summed[:, :pair] / summed[:, pair:]
                pieces.append(
                    jnp.where(low, share[:queries], share[queries:]).astype(jnp.bfloat16)
                )
            halves.append(jnp.concatenate(pieces, 1))
        attended = jnp.concatenate(halves, 0)
        summed = load_band(b, stream) + jnp.dot(attended, wo[l], preferred_element_type=f32)
        if last:
            rows = BAND * token_cols
            out[pl.ds(pl.multiple_of(b * rows, rows), rows), :] = jnp.dot(
                back, summed.astype(jnp.bfloat16), preferred_element_type=jnp.float32
            ).astype(jnp.bfloat16)
        else:
            store_band(b, summed, stream)
            store_cells(b, normed(summed, gain[l + 1 : l + 2, :]), xs.at[l + 1])
            send_band(l + 1, b)
        return carry

    for l in range(layers):
        for n in range(3):
            w_loads[l][n].wait()
            put = put_q if n == 0 else functools.partial(put_own, (n - 1) * width)
            project(xs.at[l], w.at[l, n], put)
        wait_halo(l)
        for n in (1, 2):
            project(xhs.at[l], w.at[l, n], functools.partial(put_halo, (n - 1) * width))
        w_loads[l][3].wait()
        lax.fori_loop(0, bands, functools.partial(band, l), 0)

    for src, sem in (
        (marks_out.at[: n_col - 1], place_mark_sem),
        (placed.at[:, :, : n_col - 1], place_sem),
        (counts_out.at[: n_row - 1], count_out_sem),
        (passed.at[: n_row - 1], pass_sem),
    ):
        pltpu.make_async_copy(src, src, sem).wait()


def per_device(
    scans, dest, offsets, profile_index, profiles, embed_weight, attn_gain, qkv_weight, out_weight
):
    sizes = (lax.axis_size("row"), lax.axis_size("col"))
    n_row, n_col = sizes
    blocks, strip, channels, tile_cols = scans.shape
    token_cols = tile_cols // PATCH
    count = TOK_H * token_cols
    tile_rows = TOK_H * PATCH
    profile_count = profiles.shape[0]
    depth, width = embed_weight.shape
    layers = qkv_weight.shape[0]
    capacity = max(2, 2 * blocks // (n_row * n_col))
    capacity = -(-capacity * strip // 16) * 16 // strip
    slots = strip * capacity
    group = max(1, 16 // capacity)
    parts = 2
    chunk = channels * tile_cols // parts
    f32, bf16 = jnp.float32, jnp.bfloat16

    groups = token_cols // RADIUS
    unit = RADIUS * RADIUS
    units = TOK_H // RADIUS
    halo = 2 * groups + 2 * (units + 2)
    win = BAND + 2 * RADIUS
    masks = (TOK_H // BAND, token_cols // (2 * RADIUS), 2 * BAND * RADIUS, 4 * win * RADIUS)
    dma = pltpu.SemaphoreType.DMA
    hbm = pl.BlockSpec(memory_space=pl.ANY)
    result = pl.pallas_call(
        functools.partial(whole_kernel, sizes, capacity, token_cols, parts),
        out_shape=jax.ShapeDtypeStruct((count, width), bf16),
        in_specs=[hbm, VMEM, VMEM, VMEM, VMEM, hbm, VMEM, hbm, hbm],
        out_specs=VMEM,
        scratch_shapes=[
            pltpu.VMEM((blocks * strip * channels, tile_cols), f32),
            pltpu.VMEM((depth, width), bf16),
            pltpu.VMEM((n_row, parts, n_col, slots, chunk), bf16),
            pltpu.VMEM((n_row, parts, n_col, slots, chunk), bf16),
            pltpu.VMEM((strip // group, group * blocks, channels * tile_cols), bf16),
            pltpu.VMEM((n_col, 16, 128), f32),
            pltpu.VMEM((n_col, 16, 128), f32),
            pltpu.VMEM((16, n_col * slots), f32),
            pltpu.VMEM((n_row + 1, parts, tile_rows, chunk), bf16),
            pltpu.VMEM((n_row, parts, tile_rows, chunk), bf16),
            pltpu.VMEM((n_row, profile_count, tile_rows), bf16),
            pltpu.VMEM((n_row, profile_count, tile_rows), bf16),
            pltpu.VMEM((parts, tile_rows, chunk), f32),
            pltpu.VMEM((tile_rows, tile_cols), f32),
            pltpu.VMEM((channels // parts, tile_rows, tile_cols), f32),
            pltpu.VMEM((TOK_H * tile_cols, PATCH * channels // parts), f32),
            pltpu.VMEM((parts, depth // parts, width), bf16),
            pltpu.VMEM((groups, units * unit, width), f32),
            pltpu.VMEM((layers, groups, units, unit, width), bf16),
            pltpu.VMEM((layers, halo, unit, width), bf16),
            pltpu.VMEM(masks, f32),
            pltpu.VMEM((groups, units * unit, width), bf16),
            pltpu.VMEM((groups + 2, (units + 2) * unit, 2 * width), bf16),
            pltpu.VMEM((layers, 3, width, width), bf16),
            pltpu.VMEM((layers, width, width), bf16),
            dma((2,)),
            dma((layers, 4)),
            dma,
            dma((n_row, parts)),
            dma,
            dma,
            dma((n_row, parts)),
            dma,
            dma((n_row + 1, parts)),
            dma,
            dma,
            dma((layers, 8)),
            dma((layers, 8)),
        ],
        compiler_params=pltpu.CompilerParams(
            vmem_limit_bytes=60 * 2**20, collective_id=0, has_side_effects=True
        ),
        name="whole",
    )(
        scans.reshape(blocks * strip * channels, tile_cols),
        dest.reshape(1, blocks),
        offsets.reshape(1, blocks),
        profile_index.reshape(1, blocks),
        profiles,
        embed_weight,
        attn_gain,
        qkv_weight,
        out_weight,
    )
    return result.reshape(TOK_H, token_cols, width)


def solution(mesh):
    placed = (
        P(("row", "col"), None, None, None),
        P(("row", "col"), None),
        P(("row", "col")),
        P(("row", "col")),
        P(),
        P(),
        P(),
        P(),
        P(),
    )
    return jax.shard_map(
        per_device, mesh=mesh, in_specs=placed, out_specs=P("row", "col", None), check_vma=False
    )
```

```python
import functools

import jax
import jax.numpy as jnp
from jax import lax
from jax.experimental import pallas as pl
from jax.experimental.pallas import tpu as pltpu
from jax.sharding import PartitionSpec as P

HEADS = 16
RADIUS = 4
TOK_H = 32
PATCH = 8
BAND = 8

VMEM = pl.BlockSpec(memory_space=pltpu.VMEM)


def normed(stream, gain_row):
    centre = jnp.mean(stream, -1, keepdims=True)
    spread = jnp.mean(jnp.square(stream - centre), -1, keepdims=True)
    return ((stream - centre) * lax.rsqrt(spread + 1e-05) * gain_row).astype(jnp.bfloat16)


def regroup(token_cols, back=False):
    tokens = BAND * token_cols
    each = BAND * RADIUS
    shape = (tokens, tokens)
    grouped = lax.broadcasted_iota(jnp.int32, shape, 1 if back else 0)
    natural = lax.broadcasted_iota(jnp.int32, shape, 0 if back else 1)
    inner = grouped % each
    source = inner // RADIUS * token_cols + grouped // each * RADIUS + inner % RADIUS
    return (natural == source).astype(jnp.float32).astype(jnp.bfloat16)


def store_band(b, total, stream):
    each = BAND * RADIUS
    at = pl.ds(pl.multiple_of(b * each, each), each)
    for g in range(stream.shape[0]):
        stream[g, at, :] = total[g * each : (g + 1) * each]


def load_band(b, stream):
    each = BAND * RADIUS
    at = pl.ds(pl.multiple_of(b * each, each), each)
    return jnp.concatenate([stream[g, at, :] for g in range(stream.shape[0])], 0)


def store_cells(b, cells, inputs):
    each = BAND * RADIUS
    units = each // inputs.shape[2]
    for g in range(inputs.shape[0]):
        rows = slice(g * each, (g + 1) * each)
        inputs[g, pl.ds(b * units, units)] = cells[rows].reshape(
            units, each // units, cells.shape[1]
        )


def iota(shape, dim):
    return lax.broadcasted_iota(jnp.int32, shape, dim)


def hot(mask):
    return mask.astype(jnp.float32).astype(jnp.bfloat16)


def rows_dot(a, b):
    return lax.dot_general(a, b, (((1,), (1,)), ((), ())), preferred_element_type=jnp.float32)


def exact_dot(a, b):
    return jnp.dot(a, b, precision=lax.Precision.HIGHEST, preferred_element_type=jnp.float32)


def target_of(j, z, n):
    if j == n - 1:
        return z
    low = jnp.where(n - 1 - j > z, n - 1 - j, n - 2 - j)
    high = jnp.where(z > j, j, j + 1)
    return jnp.where(2 * z < n, low, high)


def window_bias(token_cols, sizes, bias):
    win = BAND + 2 * RADIUS
    shape = bias.shape[2:]
    q, k = iota(shape, 0), iota(shape, 1)
    q_row = q % (BAND * RADIUS) // RADIUS
    q_col = q // (BAND * RADIUS) * RADIUS + q % RADIUS
    k_row = k % (win * RADIUS) // RADIUS - RADIUS
    k_col = k // (win * RADIUS) * RADIUS + k % RADIUS - RADIUS
    near = (jnp.abs(k_row - q_row) <= RADIUS) & (jnp.abs(k_col - q_col) <= RADIUS)
    for b in range(bias.shape[0]):
        g_row = lax.axis_index("row") * TOK_H + b * BAND + k_row
        row_in = near & (g_row >= 0) & (g_row < TOK_H * sizes[0])
        for s in range(bias.shape[1]):
            g_col = lax.axis_index("col") * token_cols + s * 2 * RADIUS + k_col
            inside = row_in & (g_col >= 0) & (g_col < token_cols * sizes[1])
            bias[b, s] = jnp.where(inside, 0.0, -1e30)


def whole_kernel(
    sizes, capacity, token_cols, parts,
    scans_hbm, dest, offsets, profile, profiles, embed_hbm, gain, qkv, out_w,
    out,
    scans, embed, placed, got, weighted, marks_out, marks_in, marks, carried, passed,
    counts_out, counts_in, total, den, image, turned, embed2, stream, xs, xhs, bias, q_ref, kv, w, wo,
    feed_out, feed_in, fed, fed_marks, placed_fed, got_fed,
    load_sem, w_sem, feed_send, feed_recv, fed_sem, place_sem, got_sem, place_mark_sem, mark_sem, local_sem, pass_sem,
    carry_sem, count_out_sem, count_in_sem, send, recv,
):
    n_row, n_col = sizes
    layers = w.shape[0]
    blocks = dest.shape[1]
    profile_count, strip, lanes = profiles.shape
    channels = scans.shape[0] // (blocks * strip)
    slots = strip * capacity
    group = max(1, 16 // capacity)
    chunk = channels * lanes // parts
    tile_rows = TOK_H * PATCH
    keys = n_col * slots
    bands = TOK_H // BAND
    per_part = chunk // lanes
    z, col = lax.axis_index("row"), lax.axis_index("col")
    mesh_ids = pl.DeviceIdType.MESH
    f32, bf16 = jnp.float32, jnp.bfloat16
    width = wo.shape[2]
    head_dim = width // HEADS
    groups, units, unit = xs.shape[1:4]
    own = units * unit
    count = groups * own

    loads = [
        pltpu.make_async_copy(scans_hbm, scans, load_sem.at[0]),
        pltpu.make_async_copy(embed_hbm, embed, load_sem.at[1]),
    ]
    w_loads = [
        [
            pltpu.make_async_copy(
                qkv.at[l, :, n * width : (n + 1) * width], w.at[l, n], w_sem.at[l, n]
            )
            for n in range(3)
        ]
        + [pltpu.make_async_copy(out_w.at[l], wo.at[l], w_sem.at[l, 3])]
        for l in range(layers)
    ]
    for load in loads:
        load.start()

    up, down = z > 0, z < n_row - 1
    west, east = col > 0, col < n_col - 1
    l0 = 2 * groups
    r0 = l0 + units + 2
    end = r0 + units + 2
    where = [
        (-1, 0, up), (1, 0, down), (0, -1, west), (0, 1, east),
        (-1, -1, up & west), (-1, 1, up & east), (1, -1, down & west), (1, 1, down & east),
    ]
    opposite = [1, 0, 3, 2, 7, 6, 5, 4]

    def pieces(l):
        x, xh = xs.at[l], xhs.at[l]
        top, bottom = xh.at[:groups], xh.at[groups : 2 * groups]
        left, right = xh.at[l0 + 1 : r0 - 1], xh.at[r0 + 1 : end - 1]
        return [
            (x.at[:, 0], bottom, top),
            (x.at[:, units - 1], top, bottom),
            (x.at[0], right, left),
            (x.at[groups - 1], left, right),
            (x.at[0, 0], xh.at[end - 1], xh.at[l0]),
            (x.at[groups - 1, 0], xh.at[r0 - 1], xh.at[r0]),
            (x.at[0, units - 1], xh.at[r0], xh.at[r0 - 1]),
            (x.at[groups - 1, units - 1], xh.at[l0], xh.at[end - 1]),
        ]

    def send_halo(l, n, at=None):
        dr, dc, there = where[n]
        source, lands, _ = pieces(l)[n]
        if at is not None:
            source, lands = source.at[at], lands.at[at]

        @pl.when(there)
        def _():
            pltpu.make_async_remote_copy(
                src_ref=source,
                dst_ref=lands,
                send_sem=send.at[l, n],
                recv_sem=recv.at[l, n],
                device_id=(z + dr, col + dc),
                device_id_type=mesh_ids,
            ).start()

    def send_band(l, b):
        per_band = BAND // RADIUS
        at = pl.ds(b * per_band, per_band)
        send_halo(l, 2, at)
        send_halo(l, 3, at)

        @pl.when(b == 0)
        def _():
            for n in (0, 4, 5):
                send_halo(l, n)

        @pl.when(b == bands - 1)
        def _():
            for n in (1, 6, 7):
                send_halo(l, n)

    def wait_halo(l):
        for n, (_, _, there) in enumerate(where):
            source, _, here = pieces(l)[n]

            @pl.when(there)
            def _(n=n, source=source, here=here):
                pltpu.make_async_copy(source, source, send.at[l, n]).wait()
                pltpu.make_async_copy(here, here, recv.at[l, opposite[n]]).wait()

    early = parts - 1 if n_row > 3 else parts
    outer = (z == 0) | (z == n_row - 1)
    helper = (z == 1) | (z == n_row - 2) if early < parts else z < 0
    feeder = jnp.where(z == 1, 0, n_row - 1)
    aide = jnp.where(z == 0, 1, n_row - 2)

    def to_aide(source, lands, n):
        return pltpu.make_async_remote_copy(
            src_ref=source,
            dst_ref=lands,
            send_sem=feed_send.at[n],
            recv_sem=feed_recv.at[n],
            device_id=(aide, col),
            device_id_type=mesh_ids,
        )

    barrier = pltpu.get_barrier_semaphore()
    for d in range(1, n_col):
        pl.semaphore_signal(
            barrier, inc=1, device_id=(z, lax.rem(col + d, n_col)), device_id_type=mesh_ids
        )
    for d in range(1, n_row):
        pl.semaphore_signal(
            barrier, inc=1, device_id=(lax.rem(z + d, n_row), col), device_id_type=mesh_ids
        )
    for dr, dc, there in where[4:]:

        @pl.when(there)
        def _(dr=dr, dc=dc):
            pl.semaphore_signal(
                barrier, inc=1, device_id=(z + dr, col + dc), device_id_type=mesh_ids
            )

    for l in range(layers):
        for n, (_, _, there) in enumerate(where):
            here = pieces(l)[n][2]

            @pl.when(jnp.logical_not(there))
            def _(here=here):
                here[...] = jnp.zeros(here.shape, here.dtype)

    dest_row, off_row, prof_row = dest[...], offsets[...], profile[...]
    square = jnp.broadcast_to(dest_row.astype(f32), (blocks, blocks))
    earlier = (square.T == square) & (iota((blocks, blocks), 0) < iota((blocks, blocks), 1))
    rank_row = jnp.sum(earlier.astype(f32), 0, keepdims=True).astype(jnp.int32)

    tile_shape = (n_col * 8, blocks)
    step_row = iota(tile_shape, 0) % 8
    tile = jnp.where(step_row < n_row, step_row * n_col + iota(tile_shape, 0) // 8, -1)
    to_tile = hot(tile == dest_row)
    same = iota((128, blocks), 0) % capacity == rank_row
    for n, what in enumerate((off_row, prof_row)):
        value = jnp.where(same, what + 1, 0).astype(f32).astype(bf16)
        marks_out[:, n * 8 : (n + 1) * 8, :] = rows_dot(to_tile, value).reshape(n_col, 8, 128)

    own_profile = (
        iota((blocks, blocks), 0) == jnp.broadcast_to(prof_row, (blocks, blocks))
    ).astype(f32).T[:, :profile_count]
    loads[0].wait()
    for i in range(strip):
        weight = exact_dot(own_profile, profiles[:, i, :])
        for c in range(channels):
            block_row = scans[pl.ds(i * channels + c, blocks, stride=strip * channels), :]
            at = c % per_part * lanes
            weighted[
                c // per_part,
                i // group,
                i % group * blocks : (i % group + 1) * blocks,
                at : at + lanes,
            ] = (block_row * weight).astype(bf16)

    for load in sum(w_loads, []):
        load.start()
    rows_near = up.astype(jnp.int32) + down.astype(jnp.int32)
    cols_near = west.astype(jnp.int32) + east.astype(jnp.int32)
    pl.semaphore_wait(barrier, n_col - 1 + n_row - 1 + rows_near * cols_near)

    if early < parts:
        feed_out[...] = jnp.broadcast_to(dest_row * (group * capacity) + rank_row, feed_out.shape)

        @pl.when(outer)
        def _():
            to_aide(feed_out, feed_in, 0).start()
            to_aide(weighted.at[early], fed, 1).start()

    slot_row = jnp.concatenate(
        [dest_row * (group * capacity) + ig * capacity + rank_row for ig in range(group)], 1
    )
    per_step = n_col * group * capacity
    for d in range(1, n_col):
        peer = lax.rem(col + d, n_col)
        pltpu.make_async_remote_copy(
            src_ref=marks_out.at[peer],
            dst_ref=marks_in.at[col],
            send_sem=place_mark_sem,
            recv_sem=mark_sem,
            device_id=(z, peer),
            device_id_type=mesh_ids,
        ).start()

    def place(t, pick, source, puts, takes, local, sent, seen):
        for g in range(strip // group):
            y = jnp.dot(pick, source[g], preferred_element_type=f32).astype(bf16)
            puts[:, g * group * capacity : (g + 1) * group * capacity, :] = y.reshape(
                n_col, group * capacity, chunk
            )
        pltpu.make_async_copy(puts.at[col], takes.at[col], local).start()
        for d in range(1, n_col):
            peer = lax.rem(col + d, n_col)
            pltpu.make_async_remote_copy(
                src_ref=puts.at[peer],
                dst_ref=takes.at[col],
                send_sem=sent,
                recv_sem=seen,
                device_id=(z, peer),
                device_id_type=mesh_ids,
            ).start()

    def place_own(j):
        t = target_of(j, z, n_row)
        pick = hot(iota((per_step, group * blocks), 0) + t * per_step == slot_row)
        for h in range(parts):

            def go(h=h):
                place(
                    t, pick, weighted.at[h], placed.at[t, h], got.at[t, h],
                    local_sem.at[j, h], place_sem.at[int(h == early)], got_sem.at[j, h],
                )

            if h == early and j < n_row - 1:
                pl.when(jnp.logical_not(outer))(go)
            else:
                go()

    def place_fed(j):
        t = target_of(j, z, n_row)

        @pl.when(helper & (t != feeder))
        def _():
            row = feed_in[0:1, :]
            fed_row = jnp.concatenate([row + ig * capacity for ig in range(group)], 1)
            pick = hot(iota((per_step, group * blocks), 0) + t * per_step == fed_row)
            place(
                t, pick, fed, placed_fed.at[t], got_fed.at[t],
                fed_sem.at[0, j], fed_sem.at[1, 0], fed_sem.at[2, j],
            )

    def await_fed(n, lands):
        @pl.when(helper)
        def _():
            pltpu.make_async_copy(lands, lands, feed_recv.at[n]).wait()

    for j in range(n_row):
        place_own(j)
        if early < parts and j == 1:
            await_fed(0, feed_in)
            await_fed(1, fed)
            place_fed(0)
            place_fed(1)
        if early < parts and j > 1:
            place_fed(j)

    def prepare():
        loads[1].wait()
        depth = embed.shape[0] // parts
        pick_shape = (depth, depth)
        inner = depth // PATCH
        source = iota(pick_shape, 0) % inner * PATCH + iota(pick_shape, 0) // inner
        reorder = hot(iota(pick_shape, 1) == source)
        for h in range(parts):
            for n in range(0, embed.shape[1], 512):
                embed2[h, :, n : n + 512] = jnp.dot(
                    reorder,
                    embed[h * depth : (h + 1) * depth, n : n + 512],
                    preferred_element_type=f32,
                ).astype(bf16)
        window_bias(token_cols, sizes, bias)

    def denominator():
        pltpu.make_async_copy(
            counts_in.at[: n_row - 1], counts_in.at[: n_row - 1], count_in_sem
        ).wait()
        hits = counts_in[0].astype(f32)
        for s in range(1, n_row):
            hits += counts_in[s].astype(f32)
        divisor = jnp.ones((tile_rows, lanes), f32)
        for i in range(strip):
            shifted = hits if i == 0 else pltpu.roll(hits, i, 1)
            divisor += exact_dot(shifted.T, profiles[:, i, :])
        den[...] = divisor

    part_tokens = BAND * token_cols
    order = regroup(token_cols)
    half_depth = embed_hbm.shape[0] // parts

    def embed_half(h, opening, closing):
        for c in range(per_part):
            pixels = total[h, :, c * lanes : (c + 1) * lanes] / den[...]
            image[c] = pixels.astype(bf16).astype(f32)

        def turn(i, carry):
            rows = pl.ds(pl.multiple_of(i * PATCH, PATCH), PATCH)
            block = image[:, rows, :].reshape(per_part * PATCH, lanes)
            turned[pl.ds(pl.multiple_of(i * lanes, lanes), lanes), :] = block.T
            return carry

        lax.fori_loop(0, TOK_H, turn, 0, unroll=8)

        def embed_part(n, carry):
            k = jnp.where(n == 0, 0, jnp.where(n == 1, bands - 1, n - 1)) if closing else n
            lhs = jnp.concatenate(
                [
                    turned[pl.ds(k * part_tokens * PATCH + q, part_tokens, stride=PATCH), :]
                    for q in range(PATCH)
                ],
                1,
            ).astype(bf16)
            lhs = jnp.dot(order, lhs, preferred_element_type=f32).astype(bf16)
            part = jnp.dot(lhs, embed2[h], preferred_element_type=f32)
            if not opening:
                part += load_band(k, stream)
            store_band(k, part, stream)
            if closing:
                store_cells(k, normed(part, gain[0:1, :]), xs.at[0])
                send_band(0, k)
            return carry

        lax.fori_loop(0, bands, embed_part, 0)

    pltpu.make_async_copy(
        marks_in.at[: n_col - 1], marks_in.at[: n_col - 1], mark_sem
    ).wait()
    per_tile = 128 // slots
    for u in range(keys // 128):
        mark = jnp.zeros((16, 128), f32)
        for s in range(per_tile):
            src = u * per_tile + s
            seen = jnp.where(src == col, marks_out[src], marks_in[src])
            mark = jnp.where(iota((16, 128), 1) // slots == s, seen, mark)
        marks[:, u * 128 : (u + 1) * 128] = mark
    if early < parts:

        @pl.when(outer)
        def _():
            to_aide(marks, fed_marks, 2).start()

        await_fed(2, fed_marks)
    strip_row = iota((1, keys), 1) % slots // capacity
    pixel = iota((tile_rows, keys), 0)
    for j in range(n_row):
        t = target_of(j, z, n_row)
        mark = marks[pl.ds(t, 1), :].astype(jnp.int32)
        which = marks[pl.ds(t + 8, 1), :].astype(jnp.int32)
        row_of = jnp.where(mark > 0, mark - 1 + strip_row, -1)
        spread = hot(pixel == row_of)
        first = jnp.where(strip_row == 0, which, 0)
        by_profile = hot(iota((profile_count, keys), 0) + 1 == first)
        count = rows_dot(by_profile, spread).astype(bf16)
        last = j == n_row - 1
        if j == min(1, n_row - 1):
            prepare()
        if last:
            counts_in[z] = count
        else:
            counts_out[t] = count
            pltpu.make_async_remote_copy(
                src_ref=counts_out.at[t],
                dst_ref=counts_in.at[z],
                send_sem=count_out_sem,
                recv_sem=count_in_sem,
                device_id=(t, col),
                device_id_type=mesh_ids,
            ).start()
            up = t > z
            near = jnp.where(up, z + 1, z - 1)
            slot = jnp.where(jnp.logical_not(up) & (near == t), n_row, t)
            has = jnp.where(up, z > 0, z < n_row - 1)
            has_early = jnp.where(up, z > 1, z < n_row - 2)

        def gather(h, j=j, t=t, spread=spread):
            pltpu.make_async_copy(
                placed.at[t, h, col], got.at[t, h, col], local_sem.at[j, h]
            ).wait()
            pltpu.make_async_copy(
                got.at[t, h, : n_col - 1], got.at[t, h, : n_col - 1], got_sem.at[j, h]
            ).wait()
            total[h] = jnp.dot(
                spread, got[t, h].reshape(keys, chunk), preferred_element_type=f32
            )
            if h == early:

                @pl.when(helper & (t != feeder))
                def _():
                    pltpu.make_async_copy(
                        placed_fed.at[t, col], got_fed.at[t, col], fed_sem.at[0, j]
                    ).wait()
                    some = got_fed.at[t, : n_col - 1]
                    pltpu.make_async_copy(some, some, fed_sem.at[2, j]).wait()
                    far = fed_marks[pl.ds(t, 1), :].astype(jnp.int32)
                    far_row = jnp.where(far > 0, far - 1 + strip_row, -1)
                    total[h] += jnp.dot(
                        hot(pixel == far_row),
                        got_fed[t].reshape(keys, chunk),
                        preferred_element_type=f32,
                    )

        def add(there, here, h):
            @pl.when(there)
            def _():
                pltpu.make_async_copy(
                    carried.at[here, h], carried.at[here, h], carry_sem.at[here, h]
                ).wait()
                total[h] += carried[here, h].astype(f32)

        if last:
            ranks = list(range(parts))
            if early < parts:
                ranks = [*ranks[:2], early, *ranks[2:-1]]
            for n, h in enumerate(ranks):
                gather(h)
                if n == 0:
                    denominator()
                add(z > int(h == early), z, h)
                add(z < n_row - 1 - int(h == early), n_row, h)
                embed_half(h, n == 0, n == parts - 1)
        else:
            for h in range(parts):

                def forward(h=h):
                    gather(h)
                    add(has_early if h == early else has, t, h)
                    passed[t, h] = total[h].astype(bf16)
                    pltpu.make_async_remote_copy(
                        src_ref=passed.at[t, h],
                        dst_ref=carried.at[slot, h],
                        send_sem=pass_sem.at[int(h == early)],
                        recv_sem=carry_sem.at[slot, h],
                        device_id=(near, col),
                        device_id_type=mesh_ids,
                    ).start()

                if h == early:
                    pl.when(jnp.logical_not(outer))(forward)
                else:
                    forward()

    step = 1024

    def project(rows, weight, put):
        def part(k, c):
            cols = pl.ds(pl.multiple_of(k * step, step), step)
            y = jnp.dot(
                rows[...].reshape(-1, width), weight[:, cols], preferred_element_type=f32
            ).astype(bf16)
            put(k, y)
            return c

        lax.fori_loop(0, width // step, part, 0)

    def put_q(k, y):
        cols = pl.ds(pl.multiple_of(k * step, step), step)
        for g in range(groups):
            q_ref[g, :, cols] = (y[g * own : (g + 1) * own] * head_dim ** (-0.5)).astype(
                jnp.bfloat16
            )

    def put_own(base, k, y):
        cols = pl.ds(pl.multiple_of(base + k * step, step), step)
        for g in range(groups):
            kv[g + 1, unit : unit + own, cols] = y[g * own : (g + 1) * own]

    def put_halo(base, k, y):
        cols = pl.ds(pl.multiple_of(base + k * step, step), step)
        for g in range(groups):
            kv[g + 1, :unit, cols] = y[g * unit : (g + 1) * unit]
            kv[g + 1, unit + own :, cols] = y[(groups + g) * unit : (groups + g + 1) * unit]
        kv[0, :, cols] = y[l0 * unit : r0 * unit]
        kv[groups + 1, :, cols] = y[r0 * unit :]

    each = BAND * RADIUS
    span = (BAND + 2 * RADIUS) * RADIUS
    pair = 2 * head_dim
    queries = 2 * each
    low = lax.broadcasted_iota(jnp.int32, (queries, pair), 1) < head_dim
    ones = jnp.ones((4 * span, pair), jnp.bfloat16)
    back = regroup(token_cols, True)

    def band(l, n, carry):
        last = l == layers - 1
        b = n if last else jnp.where(n == 0, 0, jnp.where(n == 1, bands - 1, n - 1))
        q_at = pl.ds(pl.multiple_of(b * each, each), each)
        k_at = pl.ds(pl.multiple_of(b * each, each), span)
        halves = []
        for s in range(groups // 2):
            half_bias = bias[b, s]
            both = jnp.concatenate([half_bias, half_bias], 0)
            pieces = []
            for h in range(HEADS // 2):
                cols = slice(h * pair, (h + 1) * pair)
                v_cols = slice(width + h * pair, width + (h + 1) * pair)
                q = jnp.concatenate([q_ref[2 * s + i, q_at, cols] for i in range(2)], 0)
                zero = jnp.zeros_like(q)
                q2 = jnp.concatenate([jnp.where(low, q, zero), jnp.where(low, zero, q)], 0)
                k = jnp.concatenate([kv[2 * s + i, k_at, cols] for i in range(4)], 0)
                v = jnp.concatenate([kv[2 * s + i, k_at, v_cols] for i in range(4)], 0)
                logits = lax.dot_general(
                    q2, k, (((1,), (1,)), ((), ())), preferred_element_type=jnp.float32
                )
                logits = logits + both
                top_logit = jnp.max(logits, -1, keepdims=True)
                weight = jnp.exp(logits - top_logit).astype(jnp.bfloat16)
                summed = jnp.dot(
                    weight, jnp.concatenate([v, ones], 1), preferred_element_type=jnp.float32
                )
                share = summed[:, :pair] / summed[:, pair:]
                pieces.append(
                    jnp.where(low, share[:queries], share[queries:]).astype(jnp.bfloat16)
                )
            halves.append(jnp.concatenate(pieces, 1))
        attended = jnp.concatenate(halves, 0)
        summed = load_band(b, stream) + jnp.dot(attended, wo[l], preferred_element_type=f32)
        if last:
            rows = BAND * token_cols
            out[pl.ds(pl.multiple_of(b * rows, rows), rows), :] = jnp.dot(
                back, summed.astype(jnp.bfloat16), preferred_element_type=jnp.float32
            ).astype(jnp.bfloat16)
        else:
            store_band(b, summed, stream)
            store_cells(b, normed(summed, gain[l + 1 : l + 2, :]), xs.at[l + 1])
            send_band(l + 1, b)
        return carry

    for l in range(layers):
        for n in range(3):
            w_loads[l][n].wait()
            put = put_q if n == 0 else functools.partial(put_own, (n - 1) * width)
            project(xs.at[l], w.at[l, n], put)
        wait_halo(l)
        for n in (1, 2):
            project(xhs.at[l], w.at[l, n], functools.partial(put_halo, (n - 1) * width))
        w_loads[l][3].wait()
        lax.fori_loop(0, bands, functools.partial(band, l), 0)

    for src, sem in (
        (marks_out.at[: n_col - 1], place_mark_sem),
        (placed.at[:, :early, : n_col - 1], place_sem.at[0]),
        (counts_out.at[: n_row - 1], count_out_sem),
        (passed.at[: n_row - 1, :early], pass_sem.at[0]),
    ):
        pltpu.make_async_copy(src, src, sem).wait()
    if early < parts:

        @pl.when(outer)
        def _():
            to_aide(feed_out, feed_in, 0).wait_send()
            to_aide(weighted.at[early], fed, 1).wait_send()
            to_aide(marks, fed_marks, 2).wait_send()
            sent = placed.at[0, early, : n_col - 1]
            pltpu.make_async_copy(sent, sent, place_sem.at[1]).wait()

        @pl.when(jnp.logical_not(outer))
        def _():
            for src, sem in (
                (placed.at[:, early, : n_col - 1], place_sem.at[1]),
                (passed.at[: n_row - 1, early], pass_sem.at[1]),
            ):
                pltpu.make_async_copy(src, src, sem).wait()

        @pl.when(helper)
        def _():
            sent = placed_fed.at[: n_row - 1, : n_col - 1]
            pltpu.make_async_copy(sent, sent, fed_sem.at[1, 0]).wait()


def per_device(
    scans, dest, offsets, profile_index, profiles, embed_weight, attn_gain, qkv_weight, out_weight
):
    sizes = (lax.axis_size("row"), lax.axis_size("col"))
    n_row, n_col = sizes
    blocks, strip, channels, tile_cols = scans.shape
    token_cols = tile_cols // PATCH
    count = TOK_H * token_cols
    tile_rows = TOK_H * PATCH
    profile_count = profiles.shape[0]
    depth, width = embed_weight.shape
    layers = qkv_weight.shape[0]
    capacity = max(2, 2 * blocks // (n_row * n_col))
    capacity = -(-capacity * strip // 16) * 16 // strip
    slots = strip * capacity
    group = max(1, 16 // capacity)
    parts = 4
    chunk = channels * tile_cols // parts
    f32, bf16 = jnp.float32, jnp.bfloat16

    groups = token_cols // RADIUS
    unit = RADIUS * RADIUS
    units = TOK_H // RADIUS
    halo = 2 * groups + 2 * (units + 2)
    win = BAND + 2 * RADIUS
    masks = (TOK_H // BAND, token_cols // (2 * RADIUS), 2 * BAND * RADIUS, 4 * win * RADIUS)
    dma = pltpu.SemaphoreType.DMA
    hbm = pl.BlockSpec(memory_space=pl.ANY)
    result = pl.pallas_call(
        functools.partial(whole_kernel, sizes, capacity, token_cols, parts),
        out_shape=jax.ShapeDtypeStruct((count, width), bf16),
        in_specs=[hbm, VMEM, VMEM, VMEM, VMEM, hbm, VMEM, hbm, hbm],
        out_specs=VMEM,
        scratch_shapes=[
            pltpu.VMEM((blocks * strip * channels, tile_cols), f32),
            pltpu.VMEM((depth, width), bf16),
            pltpu.VMEM((n_row, parts, n_col, slots, chunk), bf16),
            pltpu.VMEM((n_row, parts, n_col, slots, chunk), bf16),
            pltpu.VMEM((parts, strip // group, group * blocks, chunk), bf16),
            pltpu.VMEM((n_col, 16, 128), f32),
            pltpu.VMEM((n_col, 16, 128), f32),
            pltpu.VMEM((16, n_col * slots), f32),
            pltpu.VMEM((n_row + 1, parts, tile_rows, chunk), bf16),
            pltpu.VMEM((n_row, parts, tile_rows, chunk), bf16),
            pltpu.VMEM((n_row, profile_count, tile_rows), bf16),
            pltpu.VMEM((n_row, profile_count, tile_rows), bf16),
            pltpu.VMEM((parts, tile_rows, chunk), f32),
            pltpu.VMEM((tile_rows, tile_cols), f32),
            pltpu.VMEM((channels // parts, tile_rows, tile_cols), f32),
            pltpu.VMEM((TOK_H * tile_cols, PATCH * channels // parts), f32),
            pltpu.VMEM((parts, depth // parts, width), bf16),
            pltpu.VMEM((groups, units * unit, width), f32),
            pltpu.VMEM((layers, groups, units, unit, width), bf16),
            pltpu.VMEM((layers, halo, unit, width), bf16),
            pltpu.VMEM(masks, f32),
            pltpu.VMEM((groups, units * unit, width), bf16),
            pltpu.VMEM((groups + 2, (units + 2) * unit, 2 * width), bf16),
            pltpu.VMEM((layers, 3, width, width), bf16),
            pltpu.VMEM((layers, width, width), bf16),
            pltpu.VMEM((8, blocks), jnp.int32),
            pltpu.VMEM((8, blocks), jnp.int32),
            pltpu.VMEM((strip // group, group * blocks, chunk), bf16),
            pltpu.VMEM((16, n_col * slots), f32),
            pltpu.VMEM((n_row, n_col, slots, chunk), bf16),
            pltpu.VMEM((n_row, n_col, slots, chunk), bf16),
            dma((2,)),
            dma((layers, 4)),
            dma((3,)),
            dma((3,)),
            dma((3, n_row)),
            dma((2,)),
            dma((n_row, parts)),
            dma,
            dma,
            dma((n_row, parts)),
            dma((2,)),
            dma((n_row + 1, parts)),
            dma,
            dma,
            dma((layers, 8)),
            dma((layers, 8)),
        ],
        compiler_params=pltpu.CompilerParams(
            vmem_limit_bytes=60 * 2**20, collective_id=0, has_side_effects=True
        ),
        name="whole",
    )(
        scans.reshape(blocks * strip * channels, tile_cols),
        dest.reshape(1, blocks),
        offsets.reshape(1, blocks),
        profile_index.reshape(1, blocks),
        profiles,
        embed_weight,
        attn_gain,
        qkv_weight,
        out_weight,
    )
    return result.reshape(TOK_H, token_cols, width)


def solution(mesh):
    placed = (
        P(("row", "col"), None, None, None),
        P(("row", "col"), None),
        P(("row", "col")),
        P(("row", "col")),
        P(),
        P(),
        P(),
        P(),
        P(),
    )
    return jax.shard_map(
        per_device, mesh=mesh, in_specs=placed, out_specs=P("row", "col", None), check_vma=False
    )
```

```python
import functools

import jax
import jax.numpy as jnp
from jax import lax
from jax.experimental import pallas as pl
from jax.experimental.pallas import tpu as pltpu
from jax.sharding import PartitionSpec as P

HEADS = 16
RADIUS = 4
TOK_H = 32
PATCH = 8
BAND = 8

VMEM = pl.BlockSpec(memory_space=pltpu.VMEM)


def normed(stream, gain_row):
    centre = jnp.mean(stream, -1, keepdims=True)
    spread = jnp.mean(jnp.square(stream - centre), -1, keepdims=True)
    return ((stream - centre) * lax.rsqrt(spread + 1e-05) * gain_row).astype(jnp.bfloat16)


def regroup(token_cols, back=False):
    tokens = BAND * token_cols
    each = BAND * RADIUS
    shape = (tokens, tokens)
    grouped = lax.broadcasted_iota(jnp.int32, shape, 1 if back else 0)
    natural = lax.broadcasted_iota(jnp.int32, shape, 0 if back else 1)
    inner = grouped % each
    source = inner // RADIUS * token_cols + grouped // each * RADIUS + inner % RADIUS
    return (natural == source).astype(jnp.float32).astype(jnp.bfloat16)


def store_band(b, total, stream):
    each = BAND * RADIUS
    at = pl.ds(pl.multiple_of(b * each, each), each)
    for g in range(stream.shape[0]):
        stream[g, at, :] = total[g * each : (g + 1) * each]


def load_band(b, stream):
    each = BAND * RADIUS
    at = pl.ds(pl.multiple_of(b * each, each), each)
    return jnp.concatenate([stream[g, at, :] for g in range(stream.shape[0])], 0)


def store_cells(b, cells, inputs):
    each = BAND * RADIUS
    units = each // inputs.shape[2]
    for g in range(inputs.shape[0]):
        rows = slice(g * each, (g + 1) * each)
        inputs[g, pl.ds(b * units, units)] = cells[rows].reshape(
            units, each // units, cells.shape[1]
        )


def iota(shape, dim):
    return lax.broadcasted_iota(jnp.int32, shape, dim)


def hot(mask):
    return mask.astype(jnp.float32).astype(jnp.bfloat16)


def rows_dot(a, b):
    return lax.dot_general(a, b, (((1,), (1,)), ((), ())), preferred_element_type=jnp.float32)


def exact_dot(a, b):
    return jnp.dot(a, b, precision=lax.Precision.HIGHEST, preferred_element_type=jnp.float32)


def target_of(j, z, n):
    if j == n - 1:
        return z
    low = jnp.where(n - 1 - j > z, n - 1 - j, n - 2 - j)
    high = jnp.where(z > j, j, j + 1)
    return jnp.where(2 * z < n, low, high)


def window_bias(token_cols, sizes, bias):
    win = BAND + 2 * RADIUS
    shape = bias.shape[2:]
    q, k = iota(shape, 0), iota(shape, 1)
    q_row = q % (BAND * RADIUS) // RADIUS
    q_col = q // (BAND * RADIUS) * RADIUS + q % RADIUS
    k_row = k % (win * RADIUS) // RADIUS - RADIUS
    k_col = k // (win * RADIUS) * RADIUS + k % RADIUS - RADIUS
    near = (jnp.abs(k_row - q_row) <= RADIUS) & (jnp.abs(k_col - q_col) <= RADIUS)
    for b in range(bias.shape[0]):
        g_row = lax.axis_index("row") * TOK_H + b * BAND + k_row
        row_in = near & (g_row >= 0) & (g_row < TOK_H * sizes[0])
        for s in range(bias.shape[1]):
            g_col = lax.axis_index("col") * token_cols + s * 2 * RADIUS + k_col
            inside = row_in & (g_col >= 0) & (g_col < token_cols * sizes[1])
            bias[b, s] = jnp.where(inside, 0.0, -1e30)


def whole_kernel(
    sizes, capacity, token_cols, parts,
    scans_hbm, dest, offsets, profile, profiles, embed_hbm, gain, qkv, out_w,
    out,
    scans, embed, placed, got, weighted, marks_out, marks_in, marks, carried, passed,
    carried_early, passed_early,
    counts_out, counts_in, total, den, image, turned, embed2, stream, xs, xhs, bias, q_ref, kv, w, wo,
    feed_out, feed_in, fed, fed_marks, placed_fed, got_fed,
    load_sem, w_sem, feed_send, feed_recv, fed_sem, place_sem, got_sem, place_mark_sem, mark_sem, local_sem, pass_sem,
    carry_sem, carry_early_sem, count_out_sem, count_in_sem, send, recv,
):
    n_row, n_col = sizes
    layers = w.shape[0]
    blocks = dest.shape[1]
    profile_count, strip, lanes = profiles.shape
    channels = scans.shape[0] // (blocks * strip)
    slots = strip * capacity
    group = max(1, 16 // capacity)
    chunk = channels * lanes // parts
    tile_rows = TOK_H * PATCH
    keys = n_col * slots
    bands = TOK_H // BAND
    per_part = chunk // lanes
    z, col = lax.axis_index("row"), lax.axis_index("col")
    mesh_ids = pl.DeviceIdType.MESH
    f32, bf16 = jnp.float32, jnp.bfloat16
    width = wo.shape[2]
    head_dim = width // HEADS
    groups, units, unit = xs.shape[1:4]
    own = units * unit
    count = groups * own

    loads = [
        pltpu.make_async_copy(scans_hbm, scans, load_sem.at[0]),
        pltpu.make_async_copy(embed_hbm, embed, load_sem.at[1]),
    ]
    w_loads = [
        [
            pltpu.make_async_copy(
                qkv.at[l, :, n * width : (n + 1) * width], w.at[l, n], w_sem.at[l, n]
            )
            for n in range(3)
        ]
        + [pltpu.make_async_copy(out_w.at[l], wo.at[l], w_sem.at[l, 3])]
        for l in range(layers)
    ]
    for load in loads:
        load.start()

    up, down = z > 0, z < n_row - 1
    west, east = col > 0, col < n_col - 1
    l0 = 2 * groups
    r0 = l0 + units + 2
    end = r0 + units + 2
    where = [
        (-1, 0, up), (1, 0, down), (0, -1, west), (0, 1, east),
        (-1, -1, up & west), (-1, 1, up & east), (1, -1, down & west), (1, 1, down & east),
    ]
    opposite = [1, 0, 3, 2, 7, 6, 5, 4]

    def pieces(l):
        x, xh = xs.at[l], xhs.at[l]
        top, bottom = xh.at[:groups], xh.at[groups : 2 * groups]
        left, right = xh.at[l0 + 1 : r0 - 1], xh.at[r0 + 1 : end - 1]
        return [
            (x.at[:, 0], bottom, top),
            (x.at[:, units - 1], top, bottom),
            (x.at[0], right, left),
            (x.at[groups - 1], left, right),
            (x.at[0, 0], xh.at[end - 1], xh.at[l0]),
            (x.at[groups - 1, 0], xh.at[r0 - 1], xh.at[r0]),
            (x.at[0, units - 1], xh.at[r0], xh.at[r0 - 1]),
            (x.at[groups - 1, units - 1], xh.at[l0], xh.at[end - 1]),
        ]

    def send_halo(l, n, at=None):
        dr, dc, there = where[n]
        source, lands, _ = pieces(l)[n]
        if at is not None:
            source, lands = source.at[at], lands.at[at]

        @pl.when(there)
        def _():
            pltpu.make_async_remote_copy(
                src_ref=source,
                dst_ref=lands,
                send_sem=send.at[l, n],
                recv_sem=recv.at[l, n],
                device_id=(z + dr, col + dc),
                device_id_type=mesh_ids,
            ).start()

    def send_band(l, b):
        per_band = BAND // RADIUS
        at = pl.ds(b * per_band, per_band)
        send_halo(l, 2, at)
        send_halo(l, 3, at)

        @pl.when(jnp.equal(b, 0))
        def _():
            for n in (0, 4, 5):
                send_halo(l, n)

        @pl.when(jnp.equal(b, bands - 1))
        def _():
            for n in (1, 6, 7):
                send_halo(l, n)

    def wait_halo(l):
        for n, (_, _, there) in enumerate(where):
            source, _, here = pieces(l)[n]

            @pl.when(there)
            def _(n=n, source=source, here=here):
                pltpu.make_async_copy(source, source, send.at[l, n]).wait()
                pltpu.make_async_copy(here, here, recv.at[l, opposite[n]]).wait()

    early = carried.shape[2]
    outer = (z == 0) | (z == n_row - 1)
    helper = (z == 1) | (z == n_row - 2) if early < parts else z < 0
    feeder = jnp.where(z == 1, 0, n_row - 1)
    aide = jnp.where(z == 0, 1, n_row - 2)

    def to_aide(source, lands, n):
        return pltpu.make_async_remote_copy(
            src_ref=source,
            dst_ref=lands,
            send_sem=feed_send.at[n],
            recv_sem=feed_recv.at[n],
            device_id=(aide, col),
            device_id_type=mesh_ids,
        )

    barrier = pltpu.get_barrier_semaphore()
    for d in range(1, n_col):
        pl.semaphore_signal(
            barrier, inc=1, device_id=(z, lax.rem(col + d, n_col)), device_id_type=mesh_ids
        )
    for d in range(1, n_row):
        pl.semaphore_signal(
            barrier, inc=1, device_id=(lax.rem(z + d, n_row), col), device_id_type=mesh_ids
        )
    for dr, dc, there in where[4:]:

        @pl.when(there)
        def _(dr=dr, dc=dc):
            pl.semaphore_signal(
                barrier, inc=1, device_id=(z + dr, col + dc), device_id_type=mesh_ids
            )

    for l in range(layers):
        for n, (_, _, there) in enumerate(where):
            here = pieces(l)[n][2]

            @pl.when(jnp.logical_not(there))
            def _(here=here):
                here[...] = jnp.zeros(here.shape, here.dtype)

    dest_row, off_row, prof_row = dest[...], offsets[...], profile[...]
    square = jnp.broadcast_to(dest_row.astype(f32), (blocks, blocks))
    earlier = (square.T == square) & (iota((blocks, blocks), 0) < iota((blocks, blocks), 1))
    rank_row = jnp.sum(earlier.astype(f32), 0, keepdims=True).astype(jnp.int32)

    tile_shape = (n_col * 8, blocks)
    step_row = iota(tile_shape, 0) % 8
    tile = jnp.where(step_row < n_row, step_row * n_col + iota(tile_shape, 0) // 8, -1)
    to_tile = hot(tile == dest_row)
    same = iota((128, blocks), 0) % capacity == rank_row
    for n, what in enumerate((off_row, prof_row)):
        value = jnp.where(same, what + 1, 0).astype(f32).astype(bf16)
        marks_out[:, n * 8 : (n + 1) * 8, :] = rows_dot(to_tile, value).reshape(n_col, 8, 128)

    own_profile = (
        iota((blocks, blocks), 0) == jnp.broadcast_to(prof_row, (blocks, blocks))
    ).astype(f32).T[:, :profile_count]
    loads[0].wait()
    for i in range(strip):
        weight = exact_dot(own_profile, profiles[:, i, :])
        for c in range(channels):
            block_row = scans[pl.ds(i * channels + c, blocks, stride=strip * channels), :]
            at = c % per_part * lanes
            weighted[
                c // per_part,
                i // group,
                i % group * blocks : (i % group + 1) * blocks,
                at : at + lanes,
            ] = (block_row * weight).astype(bf16)

    for load in sum(w_loads, []):
        load.start()
    rows_near = up.astype(jnp.int32) + down.astype(jnp.int32)
    cols_near = west.astype(jnp.int32) + east.astype(jnp.int32)
    pl.semaphore_wait(barrier, n_col - 1 + n_row - 1 + rows_near * cols_near)

    if early < parts:
        feed_out[...] = jnp.broadcast_to(dest_row * (group * capacity) + rank_row, feed_out.shape)

        @pl.when(outer)
        def _():
            to_aide(feed_out, feed_in, 0).start()
            to_aide(weighted.at[early], fed, 1).start()

    slot_row = jnp.concatenate(
        [dest_row * (group * capacity) + ig * capacity + rank_row for ig in range(group)], 1
    )
    per_step = n_col * group * capacity
    for d in range(1, n_col):
        peer = lax.rem(col + d, n_col)
        pltpu.make_async_remote_copy(
            src_ref=marks_out.at[peer],
            dst_ref=marks_in.at[col],
            send_sem=place_mark_sem,
            recv_sem=mark_sem,
            device_id=(z, peer),
            device_id_type=mesh_ids,
        ).start()

    def place(t, pick, source, puts, takes, local, sent, seen):
        for g in range(strip // group):
            y = jnp.dot(pick, source[g], preferred_element_type=f32).astype(bf16)
            puts[:, g * group * capacity : (g + 1) * group * capacity, :] = y.reshape(
                n_col, group * capacity, chunk
            )
        pltpu.make_async_copy(puts.at[col], takes.at[col], local).start()
        for d in range(1, n_col):
            peer = lax.rem(col + d, n_col)
            pltpu.make_async_remote_copy(
                src_ref=puts.at[peer],
                dst_ref=takes.at[col],
                send_sem=sent,
                recv_sem=seen,
                device_id=(z, peer),
                device_id_type=mesh_ids,
            ).start()

    def place_own(j):
        t = target_of(j, z, n_row)
        pick = hot(iota((per_step, group * blocks), 0) + t * per_step == slot_row)
        for h in range(parts):

            def go(h=h):
                place(
                    t, pick, weighted.at[h], placed.at[t, h], got.at[t, h],
                    local_sem.at[j, h], place_sem.at[int(h == early)], got_sem.at[j, h],
                )

            if h == early and j < n_row - 1:
                pl.when(jnp.logical_not(outer))(go)
            else:
                go()

    def place_fed(j):
        t = target_of(j, z, n_row)

        @pl.when(helper & (t != feeder))
        def _():
            row = feed_in[0:1, :]
            fed_row = jnp.concatenate([row + ig * capacity for ig in range(group)], 1)
            pick = hot(iota((per_step, group * blocks), 0) + t * per_step == fed_row)
            place(
                t, pick, fed, placed_fed.at[t], got_fed.at[t],
                fed_sem.at[0, j], fed_sem.at[1, 0], fed_sem.at[2, j],
            )

    def await_fed(n, lands):
        @pl.when(helper)
        def _():
            pltpu.make_async_copy(lands, lands, feed_recv.at[n]).wait()

    for j in range(n_row):
        place_own(j)
        if early < parts and j == 1:
            await_fed(0, feed_in)
            await_fed(1, fed)
            place_fed(0)
            place_fed(1)
        if early < parts and j > 1:
            place_fed(j)

    def prepare():
        loads[1].wait()
        depth = embed.shape[0]
        pick_shape = (depth, depth)
        inner = depth // PATCH
        source = iota(pick_shape, 0) % inner * PATCH + iota(pick_shape, 0) // inner
        reorder = hot(iota(pick_shape, 1) == source)
        for n in range(0, embed.shape[1], 512):
            embed2[:, n : n + 512] = jnp.dot(
                reorder, embed[:, n : n + 512], preferred_element_type=f32
            ).astype(bf16)
        window_bias(token_cols, sizes, bias)

    def denominator():
        pltpu.make_async_copy(
            counts_in.at[: n_row - 1], counts_in.at[: n_row - 1], count_in_sem
        ).wait()
        hits = counts_in[0].astype(f32)
        for s in range(1, n_row):
            hits += counts_in[s].astype(f32)
        divisor = jnp.ones((tile_rows, lanes), f32)
        for i in range(strip):
            shifted = hits if i == 0 else pltpu.roll(hits, i, 1)
            divisor += exact_dot(shifted.T, profiles[:, i, :])
        den[...] = divisor

    part_tokens = BAND * token_cols
    order = regroup(token_cols)
    band_rows = BAND * PATCH

    def embed_band(k):
        rows = slice(k * band_rows, (k + 1) * band_rows)
        for c in range(channels):
            at = c % per_part * lanes
            pixels = total[(n_row - 1) % 2, c // per_part, rows, at : at + lanes] / den[rows, :]
            image[c] = pixels.astype(bf16).astype(f32)
        for i in range(BAND):
            block = image[:, i * PATCH : (i + 1) * PATCH, :].reshape(channels * PATCH, lanes)
            turned[i * lanes : (i + 1) * lanes, :] = block.T
        lhs = jnp.concatenate(
            [turned[pl.ds(q, part_tokens, stride=PATCH), :] for q in range(PATCH)], 1
        ).astype(bf16)
        lhs = jnp.dot(order, lhs, preferred_element_type=f32).astype(bf16)
        cells = jnp.dot(lhs, embed2[...], preferred_element_type=f32)
        store_band(k, cells, stream)
        store_cells(k, normed(cells, gain[0:1, :]), xs.at[0])
        send_band(0, k)

    pltpu.make_async_copy(
        marks_in.at[: n_col - 1], marks_in.at[: n_col - 1], mark_sem
    ).wait()
    per_tile = 128 // slots
    for u in range(keys // 128):
        mark = jnp.zeros((16, 128), f32)
        for s in range(per_tile):
            src = u * per_tile + s
            seen = jnp.where(src == col, marks_out[src], marks_in[src])
            mark = jnp.where(iota((16, 128), 1) // slots == s, seen, mark)
        marks[:, u * 128 : (u + 1) * 128] = mark
    if early < parts:

        @pl.when(outer)
        def _():
            to_aide(marks, fed_marks, 2).start()

        await_fed(2, fed_marks)
    strip_row = iota((1, keys), 1) % slots // capacity
    pixel = iota((tile_rows, keys), 0)

    def spread_of(table, t):
        mark = table[pl.ds(t, 1), :].astype(jnp.int32)
        return hot(pixel == jnp.where(mark > 0, mark - 1 + strip_row, -1))

    def count_of(j):
        t = target_of(j, z, n_row)
        first = jnp.where(strip_row == 0, marks[pl.ds(t + 8, 1), :].astype(jnp.int32), 0)
        by_profile = hot(iota((profile_count, keys), 0) + 1 == first)
        hits = rows_dot(by_profile, spread_of(marks, t)).astype(bf16)
        if j == n_row - 1:
            counts_in[z] = hits
            return
        counts_out[t] = hits
        pltpu.make_async_remote_copy(
            src_ref=counts_out.at[t],
            dst_ref=counts_in.at[z],
            send_sem=count_out_sem,
            recv_sem=count_in_sem,
            device_id=(t, col),
            device_id_type=mesh_ids,
        ).start()

    def gather(j, part_list):
        t = target_of(j, z, n_row)
        spread = spread_of(marks, t)
        for h in part_list:
            pltpu.make_async_copy(
                placed.at[t, h, col], got.at[t, h, col], local_sem.at[j, h]
            ).wait()
            pltpu.make_async_copy(
                got.at[t, h, : n_col - 1], got.at[t, h, : n_col - 1], got_sem.at[j, h]
            ).wait()
            total[j % 2, h] = jnp.dot(
                spread, got[t, h].reshape(keys, chunk), preferred_element_type=f32
            )
            if h == early:

                @pl.when(helper & (t != feeder))
                def _():
                    pltpu.make_async_copy(
                        placed_fed.at[t, col], got_fed.at[t, col], fed_sem.at[0, j]
                    ).wait()
                    some = got_fed.at[t, : n_col - 1]
                    pltpu.make_async_copy(some, some, fed_sem.at[2, j]).wait()
                    total[j % 2, early] += jnp.dot(
                        spread_of(fed_marks, t),
                        got_fed[t].reshape(keys, chunk),
                        preferred_element_type=f32,
                    )

    def add(there, j, here, r):
        @pl.when(there)
        def _():
            if r is None:
                lands = carried_early.at[here]
                pltpu.make_async_copy(lands, lands, carry_early_sem.at[here]).wait()
                total[j % 2, early] += carried_early[here].astype(f32)
            else:
                lands = carried.at[here, r]
                pltpu.make_async_copy(lands, lands, carry_sem.at[here, r]).wait()
                rows = slice(r * band_rows, (r + 1) * band_rows)
                total[j % 2, :early, rows, :] += carried[here, r].astype(f32)

    def forward(j, r):
        t = target_of(j, z, n_row)
        above = t > z
        near = jnp.where(above, z + 1, z - 1)
        slot = jnp.where(jnp.logical_not(above) & (near == t), n_row, t)
        margin = int(r is None)
        add(jnp.where(above, z > margin, z < n_row - 1 - margin), j, t, r)
        if r is None:
            passed_early[t] = total[j % 2, early].astype(bf16)
            source, lands = passed_early.at[t], carried_early.at[slot]
            sems = pass_sem.at[1], carry_early_sem.at[slot]
        else:
            passed[t, r] = total[j % 2, :early, r * band_rows : (r + 1) * band_rows, :].astype(bf16)
            source, lands = passed.at[t, r], carried.at[slot, r]
            sems = pass_sem.at[0], carry_sem.at[slot, r]
        pltpu.make_async_remote_copy(
            src_ref=source,
            dst_ref=lands,
            send_sem=sems[0],
            recv_sem=sems[1],
            device_id=(near, col),
            device_id_type=mesh_ids,
        ).start()

    def forward_early(j):
        if early < parts:

            @pl.when(jnp.logical_not(outer))
            def _():
                gather(j, [early])
                forward(j, None)

    band_order = [0, bands - 1, *range(1, bands - 1)]
    pairs = [list(range(j, min(j + 2, n_row - 1))) for j in range(1, n_row - 1, 2)]
    for js in [[0], *pairs]:
        for r in band_order:
            for j in js:
                if r == 0:
                    gather(j, range(early))
                forward(j, r)
            if r == (band_order[-1] if js == [0] else 0):
                for j in js:
                    forward_early(j)
        if js == [0]:
            for j in range(n_row):
                count_of(j)
            prepare()
    final = n_row - 1
    gather(final, range(early))
    denominator()
    if early < parts:
        gather(final, [early])
        add(z > 1, final, z, None)
        add(z < n_row - 2, final, n_row, None)
    for r in band_order:
        add(z > 0, final, z, r)
        add(z < n_row - 1, final, n_row, r)
        embed_band(r)

    step = 1024

    def project(rows, weight, put):
        def part(k, c):
            cols = pl.ds(pl.multiple_of(k * step, step), step)
            y = jnp.dot(
                rows[...].reshape(-1, width), weight[:, cols], preferred_element_type=f32
            ).astype(bf16)
            put(k, y)
            return c

        lax.fori_loop(0, width // step, part, 0)

    def put_q(k, y):
        cols = pl.ds(pl.multiple_of(k * step, step), step)
        for g in range(groups):
            q_ref[g, :, cols] = (y[g * own : (g + 1) * own] * head_dim ** (-0.5)).astype(
                jnp.bfloat16
            )

    def put_own(base, k, y):
        cols = pl.ds(pl.multiple_of(base + k * step, step), step)
        for g in range(groups):
            kv[g + 1, unit : unit + own, cols] = y[g * own : (g + 1) * own]

    def put_halo(base, k, y):
        cols = pl.ds(pl.multiple_of(base + k * step, step), step)
        for g in range(groups):
            kv[g + 1, :unit, cols] = y[g * unit : (g + 1) * unit]
            kv[g + 1, unit + own :, cols] = y[(groups + g) * unit : (groups + g + 1) * unit]
        kv[0, :, cols] = y[l0 * unit : r0 * unit]
        kv[groups + 1, :, cols] = y[r0 * unit :]

    each = BAND * RADIUS
    span = (BAND + 2 * RADIUS) * RADIUS
    pair = 2 * head_dim
    queries = 2 * each
    low = lax.broadcasted_iota(jnp.int32, (queries, pair), 1) < head_dim
    ones = jnp.ones((4 * span, pair), jnp.bfloat16)
    back = regroup(token_cols, True)

    def band(l, n, carry):
        last = l == layers - 1
        b = n if last else jnp.where(n == 0, 0, jnp.where(n == 1, bands - 1, n - 1))
        q_at = pl.ds(pl.multiple_of(b * each, each), each)
        k_at = pl.ds(pl.multiple_of(b * each, each), span)
        halves = []
        for s in range(groups // 2):
            half_bias = bias[b, s]
            both = jnp.concatenate([half_bias, half_bias], 0)
            pieces = []
            for h in range(HEADS // 2):
                cols = slice(h * pair, (h + 1) * pair)
                v_cols = slice(width + h * pair, width + (h + 1) * pair)
                q = jnp.concatenate([q_ref[2 * s + i, q_at, cols] for i in range(2)], 0)
                zero = jnp.zeros_like(q)
                q2 = jnp.concatenate([jnp.where(low, q, zero), jnp.where(low, zero, q)], 0)
                k = jnp.concatenate([kv[2 * s + i, k_at, cols] for i in range(4)], 0)
                v = jnp.concatenate([kv[2 * s + i, k_at, v_cols] for i in range(4)], 0)
                logits = lax.dot_general(
                    q2, k, (((1,), (1,)), ((), ())), preferred_element_type=jnp.float32
                )
                logits = logits + both
                top_logit = jnp.max(logits, -1, keepdims=True)
                weight = jnp.exp(logits - top_logit).astype(jnp.bfloat16)
                summed = jnp.dot(
                    weight, jnp.concatenate([v, ones], 1), preferred_element_type=jnp.float32
                )
                share = summed[:, :pair] / summed[:, pair:]
                pieces.append(
                    jnp.where(low, share[:queries], share[queries:]).astype(jnp.bfloat16)
                )
            halves.append(jnp.concatenate(pieces, 1))
        attended = jnp.concatenate(halves, 0)
        summed = load_band(b, stream) + jnp.dot(attended, wo[l], preferred_element_type=f32)
        if last:
            rows = BAND * token_cols
            out[pl.ds(pl.multiple_of(b * rows, rows), rows), :] = jnp.dot(
                back, summed.astype(jnp.bfloat16), preferred_element_type=jnp.float32
            ).astype(jnp.bfloat16)
        else:
            store_band(b, summed, stream)
            store_cells(b, normed(summed, gain[l + 1 : l + 2, :]), xs.at[l + 1])
            send_band(l + 1, b)
        return carry

    for l in range(layers):
        for n in range(3):
            w_loads[l][n].wait()
            put = put_q if n == 0 else functools.partial(put_own, (n - 1) * width)
            project(xs.at[l], w.at[l, n], put)
        wait_halo(l)
        for n in (1, 2):
            project(xhs.at[l], w.at[l, n], functools.partial(put_halo, (n - 1) * width))
        w_loads[l][3].wait()
        lax.fori_loop(0, bands, functools.partial(band, l), 0)

    for src, sem in (
        (marks_out.at[: n_col - 1], place_mark_sem),
        (placed.at[:, :early, : n_col - 1], place_sem.at[0]),
        (counts_out.at[: n_row - 1], count_out_sem),
        (passed.at[: n_row - 1], pass_sem.at[0]),
    ):
        pltpu.make_async_copy(src, src, sem).wait()
    if early < parts:

        @pl.when(outer)
        def _():
            to_aide(feed_out, feed_in, 0).wait_send()
            to_aide(weighted.at[early], fed, 1).wait_send()
            to_aide(marks, fed_marks, 2).wait_send()
            sent = placed.at[0, early, : n_col - 1]
            pltpu.make_async_copy(sent, sent, place_sem.at[1]).wait()

        @pl.when(jnp.logical_not(outer))
        def _():
            for src, sem in (
                (placed.at[:, early, : n_col - 1], place_sem.at[1]),
                (passed_early.at[: n_row - 1], pass_sem.at[1]),
            ):
                pltpu.make_async_copy(src, src, sem).wait()

        @pl.when(helper)
        def _():
            sent = placed_fed.at[: n_row - 1, : n_col - 1]
            pltpu.make_async_copy(sent, sent, fed_sem.at[1, 0]).wait()


def per_device(
    scans, dest, offsets, profile_index, profiles, embed_weight, attn_gain, qkv_weight, out_weight
):
    sizes = (lax.axis_size("row"), lax.axis_size("col"))
    n_row, n_col = sizes
    blocks, strip, channels, tile_cols = scans.shape
    token_cols = tile_cols // PATCH
    count = TOK_H * token_cols
    tile_rows = TOK_H * PATCH
    profile_count = profiles.shape[0]
    depth, width = embed_weight.shape
    layers = qkv_weight.shape[0]
    capacity = max(2, 2 * blocks // (n_row * n_col))
    capacity = -(-capacity * strip // 16) * 16 // strip
    slots = strip * capacity
    group = max(1, 16 // capacity)
    parts = 4
    dense = parts - 1 if n_row > 3 else parts
    bands = TOK_H // BAND
    chunk = channels * tile_cols // parts
    f32, bf16 = jnp.float32, jnp.bfloat16

    groups = token_cols // RADIUS
    unit = RADIUS * RADIUS
    units = TOK_H // RADIUS
    halo = 2 * groups + 2 * (units + 2)
    win = BAND + 2 * RADIUS
    masks = (TOK_H // BAND, token_cols // (2 * RADIUS), 2 * BAND * RADIUS, 4 * win * RADIUS)
    dma = pltpu.SemaphoreType.DMA
    hbm = pl.BlockSpec(memory_space=pl.ANY)
    result = pl.pallas_call(
        functools.partial(whole_kernel, sizes, capacity, token_cols, parts),
        out_shape=jax.ShapeDtypeStruct((count, width), bf16),
        in_specs=[hbm, VMEM, VMEM, VMEM, VMEM, hbm, VMEM, hbm, hbm],
        out_specs=VMEM,
        scratch_shapes=[
            pltpu.VMEM((blocks * strip * channels, tile_cols), f32),
            pltpu.VMEM((depth, width), bf16),
            pltpu.VMEM((n_row, parts, n_col, slots, chunk), bf16),
            pltpu.VMEM((n_row, parts, n_col, slots, chunk), bf16),
            pltpu.VMEM((parts, strip // group, group * blocks, chunk), bf16),
            pltpu.VMEM((n_col, 16, 128), f32),
            pltpu.VMEM((n_col, 16, 128), f32),
            pltpu.VMEM((16, n_col * slots), f32),
            pltpu.VMEM((n_row + 1, bands, dense, BAND * PATCH, chunk), bf16),
            pltpu.VMEM((n_row, bands, dense, BAND * PATCH, chunk), bf16),
            pltpu.VMEM((n_row + 1, tile_rows, chunk), bf16),
            pltpu.VMEM((n_row, tile_rows, chunk), bf16),
            pltpu.VMEM((n_row, profile_count, tile_rows), bf16),
            pltpu.VMEM((n_row, profile_count, tile_rows), bf16),
            pltpu.VMEM((2, parts, tile_rows, chunk), f32),
            pltpu.VMEM((tile_rows, tile_cols), f32),
            pltpu.VMEM((channels, BAND * PATCH, tile_cols), f32),
            pltpu.VMEM((BAND * tile_cols, PATCH * channels), f32),
            pltpu.VMEM((depth, width), bf16),
            pltpu.VMEM((groups, units * unit, width), f32),
            pltpu.VMEM((layers, groups, units, unit, width), bf16),
            pltpu.VMEM((layers, halo, unit, width), bf16),
            pltpu.VMEM(masks, f32),
            pltpu.VMEM((groups, units * unit, width), bf16),
            pltpu.VMEM((groups + 2, (units + 2) * unit, 2 * width), bf16),
            pltpu.VMEM((layers, 3, width, width), bf16),
            pltpu.VMEM((layers, width, width), bf16),
            pltpu.VMEM((8, blocks), jnp.int32),
            pltpu.VMEM((8, blocks), jnp.int32),
            pltpu.VMEM((strip // group, group * blocks, chunk), bf16),
            pltpu.VMEM((16, n_col * slots), f32),
            pltpu.VMEM((n_row, n_col, slots, chunk), bf16),
            pltpu.VMEM((n_row, n_col, slots, chunk), bf16),
            dma((2,)),
            dma((layers, 4)),
            dma((3,)),
            dma((3,)),
            dma((3, n_row)),
            dma((2,)),
            dma((n_row, parts)),
            dma,
            dma,
            dma((n_row, parts)),
            dma((2,)),
            dma((n_row + 1, bands)),
            dma((n_row + 1,)),
            dma,
            dma,
            dma((layers, 8)),
            dma((layers, 8)),
        ],
        compiler_params=pltpu.CompilerParams(
            vmem_limit_bytes=60 * 2**20, collective_id=0, has_side_effects=True
        ),
        name="whole",
    )(
        scans.reshape(blocks * strip * channels, tile_cols),
        dest.reshape(1, blocks),
        offsets.reshape(1, blocks),
        profile_index.reshape(1, blocks),
        profiles,
        embed_weight,
        attn_gain,
        qkv_weight,
        out_weight,
    )
    return result.reshape(TOK_H, token_cols, width)


def solution(mesh):
    placed = (
        P(("row", "col"), None, None, None),
        P(("row", "col"), None),
        P(("row", "col")),
        P(("row", "col")),
        P(),
        P(),
        P(),
        P(),
        P(),
    )
    return jax.shard_map(
        per_device, mesh=mesh, in_specs=placed, out_specs=P("row", "col", None), check_vma=False
    )
```

```python
import functools

import jax
import jax.numpy as jnp
from jax import lax
from jax.experimental import pallas as pl
from jax.experimental.pallas import tpu as pltpu
from jax.sharding import PartitionSpec as P

HEADS = 16
RADIUS = 4
TOK_H = 32
PATCH = 8
BAND = 8

VMEM = pl.BlockSpec(memory_space=pltpu.VMEM)


def normed(stream, gain_row):
    centre = jnp.mean(stream, -1, keepdims=True)
    spread = jnp.mean(jnp.square(stream - centre), -1, keepdims=True)
    return ((stream - centre) * lax.rsqrt(spread + 1e-05) * gain_row).astype(jnp.bfloat16)


def regroup(token_cols, back=False):
    tokens = BAND * token_cols
    each = BAND * RADIUS
    shape = (tokens, tokens)
    grouped = lax.broadcasted_iota(jnp.int32, shape, 1 if back else 0)
    natural = lax.broadcasted_iota(jnp.int32, shape, 0 if back else 1)
    inner = grouped % each
    source = inner // RADIUS * token_cols + grouped // each * RADIUS + inner % RADIUS
    return (natural == source).astype(jnp.float32).astype(jnp.bfloat16)


def store_band(b, total, stream):
    each = BAND * RADIUS
    at = pl.ds(pl.multiple_of(b * each, each), each)
    for g in range(stream.shape[0]):
        stream[g, at, :] = total[g * each : (g + 1) * each]


def load_band(b, stream):
    each = BAND * RADIUS
    at = pl.ds(pl.multiple_of(b * each, each), each)
    return jnp.concatenate([stream[g, at, :] for g in range(stream.shape[0])], 0)


def store_cells(b, cells, inputs):
    each = BAND * RADIUS
    units = each // inputs.shape[2]
    for g in range(inputs.shape[0]):
        rows = slice(g * each, (g + 1) * each)
        inputs[g, pl.ds(b * units, units)] = cells[rows].reshape(
            units, each // units, cells.shape[1]
        )


def iota(shape, dim):
    return lax.broadcasted_iota(jnp.int32, shape, dim)


def hot(mask):
    return mask.astype(jnp.float32).astype(jnp.bfloat16)


def rows_dot(a, b):
    return lax.dot_general(a, b, (((1,), (1,)), ((), ())), preferred_element_type=jnp.float32)


def exact_dot(a, b):
    return jnp.dot(a, b, precision=lax.Precision.HIGHEST, preferred_element_type=jnp.float32)


def target_of(j, z, n):
    if j == n - 1:
        return z
    low = jnp.where(n - 1 - j > z, n - 1 - j, n - 2 - j)
    high = jnp.where(z > j, j, j + 1)
    return jnp.where(2 * z < n, low, high)


def window_bias(token_cols, sizes, bias):
    win = BAND + 2 * RADIUS
    shape = bias.shape[2:]
    q, k = iota(shape, 0), iota(shape, 1)
    q_row = q % (BAND * RADIUS) // RADIUS
    q_col = q // (BAND * RADIUS) * RADIUS + q % RADIUS
    k_row = k % (win * RADIUS) // RADIUS - RADIUS
    k_col = k // (win * RADIUS) * RADIUS + k % RADIUS - RADIUS
    near = (jnp.abs(k_row - q_row) <= RADIUS) & (jnp.abs(k_col - q_col) <= RADIUS)
    for b in range(bias.shape[0]):
        g_row = lax.axis_index("row") * TOK_H + b * BAND + k_row
        row_in = near & (g_row >= 0) & (g_row < TOK_H * sizes[0])
        for s in range(bias.shape[1]):
            g_col = lax.axis_index("col") * token_cols + s * 2 * RADIUS + k_col
            inside = row_in & (g_col >= 0) & (g_col < token_cols * sizes[1])
            bias[b, s] = jnp.where(inside, 0.0, -1e30)


def whole_kernel(
    sizes, capacity, token_cols, parts,
    scans_hbm, dest, offsets, profile, profiles, embed_hbm, gain, qkv, out_w,
    out,
    scans, embed, placed, got, weighted, marks_out, marks_in, marks, carried, passed,
    carried_early, passed_early,
    counts_out, counts_in, total, den, image, turned, embed2, stream, xs, xhs, bias, q_ref, kv, w, wo,
    feed_out, feed_in, fed, fed_marks, placed_fed, got_fed,
    load_sem, w_sem, feed_send, feed_recv, fed_sem, place_sem, got_sem, place_mark_sem, mark_sem, local_sem, pass_sem,
    carry_sem, carry_early_sem, count_out_sem, count_in_sem, send, recv,
):
    n_row, n_col = sizes
    layers = w.shape[0]
    blocks = dest.shape[1]
    profile_count, strip, lanes = profiles.shape
    channels = scans.shape[0] // (blocks * strip)
    slots = strip * capacity
    group = max(1, 16 // capacity)
    chunk = channels * lanes // parts
    tile_rows = TOK_H * PATCH
    keys = n_col * slots
    bands = TOK_H // BAND
    per_part = chunk // lanes
    z, col = lax.axis_index("row"), lax.axis_index("col")
    mesh_ids = pl.DeviceIdType.MESH
    f32, bf16 = jnp.float32, jnp.bfloat16
    width = wo.shape[2]
    head_dim = width // HEADS
    groups, units, unit = xs.shape[1:4]
    own = units * unit
    count = groups * own

    loads = [
        pltpu.make_async_copy(scans_hbm, scans, load_sem.at[0]),
        pltpu.make_async_copy(embed_hbm, embed, load_sem.at[1]),
    ]
    w_loads = [
        [
            pltpu.make_async_copy(
                qkv.at[l, :, n * width : (n + 1) * width], w.at[l, n], w_sem.at[l, n]
            )
            for n in range(3)
        ]
        + [pltpu.make_async_copy(out_w.at[l], wo.at[l], w_sem.at[l, 3])]
        for l in range(layers)
    ]
    for load in loads:
        load.start()

    up, down = z > 0, z < n_row - 1
    west, east = col > 0, col < n_col - 1
    l0 = 2 * groups
    r0 = l0 + units + 2
    end = r0 + units + 2
    where = [
        (-1, 0, up), (1, 0, down), (0, -1, west), (0, 1, east),
        (-1, -1, up & west), (-1, 1, up & east), (1, -1, down & west), (1, 1, down & east),
    ]
    opposite = [1, 0, 3, 2, 7, 6, 5, 4]

    def pieces(l):
        x, xh = xs.at[l], xhs.at[l]
        top, bottom = xh.at[:groups], xh.at[groups : 2 * groups]
        left, right = xh.at[l0 + 1 : r0 - 1], xh.at[r0 + 1 : end - 1]
        return [
            (x.at[:, 0], bottom, top),
            (x.at[:, units - 1], top, bottom),
            (x.at[0], right, left),
            (x.at[groups - 1], left, right),
            (x.at[0, 0], xh.at[end - 1], xh.at[l0]),
            (x.at[groups - 1, 0], xh.at[r0 - 1], xh.at[r0]),
            (x.at[0, units - 1], xh.at[r0], xh.at[r0 - 1]),
            (x.at[groups - 1, units - 1], xh.at[l0], xh.at[end - 1]),
        ]

    def send_halo(l, n, at=None):
        dr, dc, there = where[n]
        source, lands, _ = pieces(l)[n]
        if at is not None:
            source, lands = source.at[at], lands.at[at]

        @pl.when(there)
        def _():
            pltpu.make_async_remote_copy(
                src_ref=source,
                dst_ref=lands,
                send_sem=send.at[l, n],
                recv_sem=recv.at[l, n],
                device_id=(z + dr, col + dc),
                device_id_type=mesh_ids,
            ).start()

    def send_band(l, b):
        per_band = BAND // RADIUS
        at = pl.ds(b * per_band, per_band)
        send_halo(l, 2, at)
        send_halo(l, 3, at)

        @pl.when(jnp.equal(b, 0))
        def _():
            for n in (0, 4, 5):
                send_halo(l, n)

        @pl.when(jnp.equal(b, bands - 1))
        def _():
            for n in (1, 6, 7):
                send_halo(l, n)

    def wait_halo(l):
        for n, (_, _, there) in enumerate(where):
            source, _, here = pieces(l)[n]

            @pl.when(there)
            def _(n=n, source=source, here=here):
                pltpu.make_async_copy(source, source, send.at[l, n]).wait()
                pltpu.make_async_copy(here, here, recv.at[l, opposite[n]]).wait()

    early = carried.shape[2]
    outer = (z == 0) | (z == n_row - 1)
    helper = (z == 1) | (z == n_row - 2) if early < parts else z < 0
    feeder = jnp.where(z == 1, 0, n_row - 1)
    aide = jnp.where(z == 0, 1, n_row - 2)

    def to_aide(source, lands, n):
        return pltpu.make_async_remote_copy(
            src_ref=source,
            dst_ref=lands,
            send_sem=feed_send.at[n],
            recv_sem=feed_recv.at[n],
            device_id=(aide, col),
            device_id_type=mesh_ids,
        )

    barrier = pltpu.get_barrier_semaphore()
    for d in range(1, n_col):
        pl.semaphore_signal(
            barrier, inc=1, device_id=(z, lax.rem(col + d, n_col)), device_id_type=mesh_ids
        )
    for d in range(1, n_row):
        pl.semaphore_signal(
            barrier, inc=1, device_id=(lax.rem(z + d, n_row), col), device_id_type=mesh_ids
        )
    for dr, dc, there in where[4:]:

        @pl.when(there)
        def _(dr=dr, dc=dc):
            pl.semaphore_signal(
                barrier, inc=1, device_id=(z + dr, col + dc), device_id_type=mesh_ids
            )

    for l in range(layers):
        for n, (_, _, there) in enumerate(where):
            here = pieces(l)[n][2]

            @pl.when(jnp.logical_not(there))
            def _(here=here):
                here[...] = jnp.zeros(here.shape, here.dtype)

    dest_row, off_row, prof_row = dest[...], offsets[...], profile[...]
    square = jnp.broadcast_to(dest_row.astype(f32), (blocks, blocks))
    earlier = (square.T == square) & (iota((blocks, blocks), 0) < iota((blocks, blocks), 1))
    rank_row = jnp.sum(earlier.astype(f32), 0, keepdims=True).astype(jnp.int32)

    tile_shape = (n_col * 8, blocks)
    step_row = iota(tile_shape, 0) % 8
    tile = jnp.where(step_row < n_row, step_row * n_col + iota(tile_shape, 0) // 8, -1)
    to_tile = hot(tile == dest_row)
    same = iota((128, blocks), 0) % capacity == rank_row
    for n, what in enumerate((off_row, prof_row)):
        value = jnp.where(same, what + 1, 0).astype(f32).astype(bf16)
        marks_out[:, n * 8 : (n + 1) * 8, :] = rows_dot(to_tile, value).reshape(n_col, 8, 128)

    own_profile = (
        iota((blocks, blocks), 0) == jnp.broadcast_to(prof_row, (blocks, blocks))
    ).astype(f32).T[:, :profile_count]
    loads[0].wait()
    for i in range(strip):
        weight = exact_dot(own_profile, profiles[:, i, :])
        for c in range(channels):
            block_row = scans[pl.ds(i * channels + c, blocks, stride=strip * channels), :]
            at = c % per_part * lanes
            weighted[
                c // per_part,
                i // group,
                i % group * blocks : (i % group + 1) * blocks,
                at : at + lanes,
            ] = (block_row * weight).astype(bf16)

    for load in sum(w_loads, []):
        load.start()
    rows_near = up.astype(jnp.int32) + down.astype(jnp.int32)
    cols_near = west.astype(jnp.int32) + east.astype(jnp.int32)
    pl.semaphore_wait(barrier, n_col - 1 + n_row - 1 + rows_near * cols_near)

    if early < parts:
        feed_out[...] = jnp.broadcast_to(dest_row * (group * capacity) + rank_row, feed_out.shape)

        @pl.when(outer)
        def _():
            to_aide(feed_out, feed_in, 0).start()
            to_aide(weighted.at[early], fed, 1).start()

    slot_row = jnp.concatenate(
        [dest_row * (group * capacity) + ig * capacity + rank_row for ig in range(group)], 1
    )
    per_step = n_col * group * capacity
    for d in range(1, n_col):
        peer = lax.rem(col + d, n_col)
        pltpu.make_async_remote_copy(
            src_ref=marks_out.at[peer],
            dst_ref=marks_in.at[col],
            send_sem=place_mark_sem,
            recv_sem=mark_sem,
            device_id=(z, peer),
            device_id_type=mesh_ids,
        ).start()

    def place(t, pick, source, puts, takes, local, sent, seen):
        for g in range(strip // group):
            y = jnp.dot(pick, source[g], preferred_element_type=f32).astype(bf16)
            puts[:, g * group * capacity : (g + 1) * group * capacity, :] = y.reshape(
                n_col, group * capacity, chunk
            )
        pltpu.make_async_copy(puts.at[col], takes.at[col], local).start()
        for d in range(1, n_col):
            peer = lax.rem(col + d, n_col)
            pltpu.make_async_remote_copy(
                src_ref=puts.at[peer],
                dst_ref=takes.at[col],
                send_sem=sent,
                recv_sem=seen,
                device_id=(z, peer),
                device_id_type=mesh_ids,
            ).start()

    def place_own(j):
        t = target_of(j, z, n_row)
        pick = hot(iota((per_step, group * blocks), 0) + t * per_step == slot_row)
        for h in range(parts):

            def go(h=h):
                place(
                    t, pick, weighted.at[h], placed.at[t, h], got.at[t, h],
                    local_sem.at[j, h], place_sem.at[int(h == early)], got_sem.at[j, h],
                )

            if h == early and j < n_row - 1:
                pl.when(jnp.logical_not(outer))(go)
            else:
                go()

    def place_fed(j):
        t = target_of(j, z, n_row)

        @pl.when(helper & (t != feeder))
        def _():
            row = feed_in[0:1, :]
            fed_row = jnp.concatenate([row + ig * capacity for ig in range(group)], 1)
            pick = hot(iota((per_step, group * blocks), 0) + t * per_step == fed_row)
            place(
                t, pick, fed, placed_fed.at[t], got_fed.at[t],
                fed_sem.at[0, j], fed_sem.at[1, 0], fed_sem.at[2, j],
            )

    def await_fed(n, lands):
        @pl.when(helper)
        def _():
            pltpu.make_async_copy(lands, lands, feed_recv.at[n]).wait()

    for j in range(n_row):
        place_own(j)
        if early < parts and j == 1:
            await_fed(0, feed_in)
            await_fed(1, fed)
            place_fed(0)
            place_fed(1)
        if early < parts and j > 1:
            place_fed(j)

    def prepare():
        loads[1].wait()
        depth = embed.shape[0]
        pick_shape = (depth, depth)
        inner = depth // PATCH
        source = iota(pick_shape, 0) % inner * PATCH + iota(pick_shape, 0) // inner
        reorder = hot(iota(pick_shape, 1) == source)
        for n in range(0, embed.shape[1], 512):
            embed2[:, n : n + 512] = jnp.dot(
                reorder, embed[:, n : n + 512], preferred_element_type=f32
            ).astype(bf16)
        window_bias(token_cols, sizes, bias)

    def denominator():
        pltpu.make_async_copy(
            counts_in.at[: n_row - 1], counts_in.at[: n_row - 1], count_in_sem
        ).wait()
        hits = counts_in[0].astype(f32)
        for s in range(1, n_row):
            hits += counts_in[s].astype(f32)
        divisor = jnp.ones((tile_rows, lanes), f32)
        for i in range(strip):
            shifted = hits if i == 0 else pltpu.roll(hits, i, 1)
            divisor += exact_dot(shifted.T, profiles[:, i, :])
        den[...] = divisor

    part_tokens = BAND * token_cols
    order = regroup(token_cols)
    prepare()
    band_rows = BAND * PATCH

    def embed_band(k):
        rows = slice(k * band_rows, (k + 1) * band_rows)
        for c in range(channels):
            at = c % per_part * lanes
            pixels = total[(n_row - 1) % 2, c // per_part, rows, at : at + lanes] / den[rows, :]
            image[c] = pixels.astype(bf16).astype(f32)
        for i in range(BAND):
            block = image[:, i * PATCH : (i + 1) * PATCH, :].reshape(channels * PATCH, lanes)
            turned[i * lanes : (i + 1) * lanes, :] = block.T
        lhs = jnp.concatenate(
            [turned[pl.ds(q, part_tokens, stride=PATCH), :] for q in range(PATCH)], 1
        ).astype(bf16)
        lhs = jnp.dot(order, lhs, preferred_element_type=f32).astype(bf16)
        cells = jnp.dot(lhs, embed2[...], preferred_element_type=f32)
        store_band(k, cells, stream)
        store_cells(k, normed(cells, gain[0:1, :]), xs.at[0])
        send_band(0, k)

    pltpu.make_async_copy(
        marks_in.at[: n_col - 1], marks_in.at[: n_col - 1], mark_sem
    ).wait()
    per_tile = 128 // slots
    for u in range(keys // 128):
        mark = jnp.zeros((16, 128), f32)
        for s in range(per_tile):
            src = u * per_tile + s
            seen = jnp.where(src == col, marks_out[src], marks_in[src])
            mark = jnp.where(iota((16, 128), 1) // slots == s, seen, mark)
        marks[:, u * 128 : (u + 1) * 128] = mark
    if early < parts:

        @pl.when(outer)
        def _():
            to_aide(marks, fed_marks, 2).start()

        await_fed(2, fed_marks)
    strip_row = iota((1, keys), 1) % slots // capacity
    pixel = iota((tile_rows, keys), 0)

    def spread_of(table, t):
        mark = table[pl.ds(t, 1), :].astype(jnp.int32)
        return hot(pixel == jnp.where(mark > 0, mark - 1 + strip_row, -1))

    def count_of(j):
        t = target_of(j, z, n_row)
        first = jnp.where(strip_row == 0, marks[pl.ds(t + 8, 1), :].astype(jnp.int32), 0)
        by_profile = hot(iota((profile_count, keys), 0) + 1 == first)
        hits = rows_dot(by_profile, spread_of(marks, t)).astype(bf16)
        if j == n_row - 1:
            counts_in[z] = hits
            return
        counts_out[t] = hits
        pltpu.make_async_remote_copy(
            src_ref=counts_out.at[t],
            dst_ref=counts_in.at[z],
            send_sem=count_out_sem,
            recv_sem=count_in_sem,
            device_id=(t, col),
            device_id_type=mesh_ids,
        ).start()

    def gather(j, part_list):
        t = target_of(j, z, n_row)
        spread = spread_of(marks, t)
        for h in part_list:
            pltpu.make_async_copy(
                placed.at[t, h, col], got.at[t, h, col], local_sem.at[j, h]
            ).wait()
            pltpu.make_async_copy(
                got.at[t, h, : n_col - 1], got.at[t, h, : n_col - 1], got_sem.at[j, h]
            ).wait()
            total[j % 2, h] = jnp.dot(
                spread, got[t, h].reshape(keys, chunk), preferred_element_type=f32
            )
            if h == early:

                @pl.when(helper & (t != feeder))
                def _():
                    pltpu.make_async_copy(
                        placed_fed.at[t, col], got_fed.at[t, col], fed_sem.at[0, j]
                    ).wait()
                    some = got_fed.at[t, : n_col - 1]
                    pltpu.make_async_copy(some, some, fed_sem.at[2, j]).wait()
                    total[j % 2, early] += jnp.dot(
                        spread_of(fed_marks, t),
                        got_fed[t].reshape(keys, chunk),
                        preferred_element_type=f32,
                    )

    def add(there, j, here, r):
        @pl.when(there)
        def _():
            if r is None:
                lands = carried_early.at[here]
                pltpu.make_async_copy(lands, lands, carry_early_sem.at[here]).wait()
                total[j % 2, early] += carried_early[here].astype(f32)
            else:
                lands = carried.at[here, r]
                pltpu.make_async_copy(lands, lands, carry_sem.at[here, r]).wait()
                rows = slice(r * band_rows, (r + 1) * band_rows)
                total[j % 2, :early, rows, :] += carried[here, r].astype(f32)

    def forward(j, r):
        t = target_of(j, z, n_row)
        above = t > z
        near = jnp.where(above, z + 1, z - 1)
        slot = jnp.where(jnp.logical_not(above) & (near == t), n_row, t)
        margin = int(r is None)
        add(jnp.where(above, z > margin, z < n_row - 1 - margin), j, t, r)
        if r is None:
            passed_early[t] = total[j % 2, early].astype(bf16)
            source, lands = passed_early.at[t], carried_early.at[slot]
            sems = pass_sem.at[1], carry_early_sem.at[slot]
        else:
            passed[t, r] = total[j % 2, :early, r * band_rows : (r + 1) * band_rows, :].astype(bf16)
            source, lands = passed.at[t, r], carried.at[slot, r]
            sems = pass_sem.at[0], carry_sem.at[slot, r]
        pltpu.make_async_remote_copy(
            src_ref=source,
            dst_ref=lands,
            send_sem=sems[0],
            recv_sem=sems[1],
            device_id=(near, col),
            device_id_type=mesh_ids,
        ).start()

    def forward_early(j):
        if early < parts:

            @pl.when(jnp.logical_not(outer))
            def _():
                gather(j, [early])
                forward(j, None)

    band_order = [0, bands - 1, *range(1, bands - 1)]
    for j in range(n_row):
        count_of(j)
    pairs = [list(range(j, min(j + 2, n_row - 1))) for j in range(1, n_row - 1, 2)]
    for js in [[0], *pairs]:
        for r in band_order:
            for j in js:
                if r == 0:
                    gather(j, range(early))
                forward(j, r)
            if r == (band_order[-1] if js == [0] else 0):
                for j in js:
                    forward_early(j)
    final = n_row - 1
    denominator()
    gather(final, range(early))
    if early < parts:
        gather(final, [early])
        add(z > 1, final, z, None)
        add(z < n_row - 2, final, n_row, None)
    for r in band_order:
        add(z > 0, final, z, r)
        add(z < n_row - 1, final, n_row, r)
        embed_band(r)

    step = 1024

    def project(rows, weight, put):
        def part(k, c):
            cols = pl.ds(pl.multiple_of(k * step, step), step)
            y = jnp.dot(
                rows[...].reshape(-1, width), weight[:, cols], preferred_element_type=f32
            ).astype(bf16)
            put(k, y)
            return c

        lax.fori_loop(0, width // step, part, 0)

    def put_q(k, y):
        cols = pl.ds(pl.multiple_of(k * step, step), step)
        for g in range(groups):
            q_ref[g, :, cols] = (y[g * own : (g + 1) * own] * head_dim ** (-0.5)).astype(
                jnp.bfloat16
            )

    def put_own(base, k, y):
        cols = pl.ds(pl.multiple_of(base + k * step, step), step)
        for g in range(groups):
            kv[g + 1, unit : unit + own, cols] = y[g * own : (g + 1) * own]

    def put_halo(base, k, y):
        cols = pl.ds(pl.multiple_of(base + k * step, step), step)
        for g in range(groups):
            kv[g + 1, :unit, cols] = y[g * unit : (g + 1) * unit]
            kv[g + 1, unit + own :, cols] = y[(groups + g) * unit : (groups + g + 1) * unit]
        kv[0, :, cols] = y[l0 * unit : r0 * unit]
        kv[groups + 1, :, cols] = y[r0 * unit :]

    each = BAND * RADIUS
    span = (BAND + 2 * RADIUS) * RADIUS
    pair = 2 * head_dim
    queries = 2 * each
    low = lax.broadcasted_iota(jnp.int32, (queries, pair), 1) < head_dim
    ones = jnp.ones((4 * span, pair), jnp.bfloat16)
    back = regroup(token_cols, True)

    def band(l, n, carry):
        last = l == layers - 1
        b = n if last else jnp.where(n == 0, 0, jnp.where(n == 1, bands - 1, n - 1))
        q_at = pl.ds(pl.multiple_of(b * each, each), each)
        k_at = pl.ds(pl.multiple_of(b * each, each), span)
        halves = []
        for s in range(groups // 2):
            half_bias = bias[b, s]
            both = jnp.concatenate([half_bias, half_bias], 0)
            pieces = []
            for h in range(HEADS // 2):
                cols = slice(h * pair, (h + 1) * pair)
                v_cols = slice(width + h * pair, width + (h + 1) * pair)
                q = jnp.concatenate([q_ref[2 * s + i, q_at, cols] for i in range(2)], 0)
                zero = jnp.zeros_like(q)
                q2 = jnp.concatenate([jnp.where(low, q, zero), jnp.where(low, zero, q)], 0)
                k = jnp.concatenate([kv[2 * s + i, k_at, cols] for i in range(4)], 0)
                v = jnp.concatenate([kv[2 * s + i, k_at, v_cols] for i in range(4)], 0)
                logits = lax.dot_general(
                    q2, k, (((1,), (1,)), ((), ())), preferred_element_type=jnp.float32
                )
                logits = logits + both
                top_logit = jnp.max(logits, -1, keepdims=True)
                weight = jnp.exp(logits - top_logit).astype(jnp.bfloat16)
                summed = jnp.dot(
                    weight, jnp.concatenate([v, ones], 1), preferred_element_type=jnp.float32
                )
                share = summed[:, :pair] / summed[:, pair:]
                pieces.append(
                    jnp.where(low, share[:queries], share[queries:]).astype(jnp.bfloat16)
                )
            halves.append(jnp.concatenate(pieces, 1))
        attended = jnp.concatenate(halves, 0)
        summed = load_band(b, stream) + jnp.dot(attended, wo[l], preferred_element_type=f32)
        if last:
            rows = BAND * token_cols
            out[pl.ds(pl.multiple_of(b * rows, rows), rows), :] = jnp.dot(
                back, summed.astype(jnp.bfloat16), preferred_element_type=jnp.float32
            ).astype(jnp.bfloat16)
        else:
            store_band(b, summed, stream)
            store_cells(b, normed(summed, gain[l + 1 : l + 2, :]), xs.at[l + 1])
            send_band(l + 1, b)
        return carry

    for l in range(layers):
        for n in range(3):
            w_loads[l][n].wait()
            put = put_q if n == 0 else functools.partial(put_own, (n - 1) * width)
            project(xs.at[l], w.at[l, n], put)
        wait_halo(l)
        for n in (1, 2):
            project(xhs.at[l], w.at[l, n], functools.partial(put_halo, (n - 1) * width))
        w_loads[l][3].wait()
        lax.fori_loop(0, bands, functools.partial(band, l), 0)

    for src, sem in (
        (marks_out.at[: n_col - 1], place_mark_sem),
        (placed.at[:, :early, : n_col - 1], place_sem.at[0]),
        (counts_out.at[: n_row - 1], count_out_sem),
        (passed.at[: n_row - 1], pass_sem.at[0]),
    ):
        pltpu.make_async_copy(src, src, sem).wait()
    if early < parts:

        @pl.when(outer)
        def _():
            to_aide(feed_out, feed_in, 0).wait_send()
            to_aide(weighted.at[early], fed, 1).wait_send()
            to_aide(marks, fed_marks, 2).wait_send()
            sent = placed.at[0, early, : n_col - 1]
            pltpu.make_async_copy(sent, sent, place_sem.at[1]).wait()

        @pl.when(jnp.logical_not(outer))
        def _():
            for src, sem in (
                (placed.at[:, early, : n_col - 1], place_sem.at[1]),
                (passed_early.at[: n_row - 1], pass_sem.at[1]),
            ):
                pltpu.make_async_copy(src, src, sem).wait()

        @pl.when(helper)
        def _():
            sent = placed_fed.at[: n_row - 1, : n_col - 1]
            pltpu.make_async_copy(sent, sent, fed_sem.at[1, 0]).wait()


def per_device(
    scans, dest, offsets, profile_index, profiles, embed_weight, attn_gain, qkv_weight, out_weight
):
    sizes = (lax.axis_size("row"), lax.axis_size("col"))
    n_row, n_col = sizes
    blocks, strip, channels, tile_cols = scans.shape
    token_cols = tile_cols // PATCH
    count = TOK_H * token_cols
    tile_rows = TOK_H * PATCH
    profile_count = profiles.shape[0]
    depth, width = embed_weight.shape
    layers = qkv_weight.shape[0]
    capacity = max(2, 2 * blocks // (n_row * n_col))
    capacity = -(-capacity * strip // 16) * 16 // strip
    slots = strip * capacity
    group = max(1, 16 // capacity)
    parts = 4
    dense = parts - 1 if n_row > 3 else parts
    bands = TOK_H // BAND
    chunk = channels * tile_cols // parts
    f32, bf16 = jnp.float32, jnp.bfloat16

    groups = token_cols // RADIUS
    unit = RADIUS * RADIUS
    units = TOK_H // RADIUS
    halo = 2 * groups + 2 * (units + 2)
    win = BAND + 2 * RADIUS
    masks = (TOK_H // BAND, token_cols // (2 * RADIUS), 2 * BAND * RADIUS, 4 * win * RADIUS)
    dma = pltpu.SemaphoreType.DMA
    hbm = pl.BlockSpec(memory_space=pl.ANY)
    result = pl.pallas_call(
        functools.partial(whole_kernel, sizes, capacity, token_cols, parts),
        out_shape=jax.ShapeDtypeStruct((count, width), bf16),
        in_specs=[hbm, VMEM, VMEM, VMEM, VMEM, hbm, VMEM, hbm, hbm],
        out_specs=VMEM,
        scratch_shapes=[
            pltpu.VMEM((blocks * strip * channels, tile_cols), f32),
            pltpu.VMEM((depth, width), bf16),
            pltpu.VMEM((n_row, parts, n_col, slots, chunk), bf16),
            pltpu.VMEM((n_row, parts, n_col, slots, chunk), bf16),
            pltpu.VMEM((parts, strip // group, group * blocks, chunk), bf16),
            pltpu.VMEM((n_col, 16, 128), f32),
            pltpu.VMEM((n_col, 16, 128), f32),
            pltpu.VMEM((16, n_col * slots), f32),
            pltpu.VMEM((n_row + 1, bands, dense, BAND * PATCH, chunk), bf16),
            pltpu.VMEM((n_row, bands, dense, BAND * PATCH, chunk), bf16),
            pltpu.VMEM((n_row + 1, tile_rows, chunk), bf16),
            pltpu.VMEM((n_row, tile_rows, chunk), bf16),
            pltpu.VMEM((n_row, profile_count, tile_rows), bf16),
            pltpu.VMEM((n_row, profile_count, tile_rows), bf16),
            pltpu.VMEM((2, parts, tile_rows, chunk), f32),
            pltpu.VMEM((tile_rows, tile_cols), f32),
            pltpu.VMEM((channels, BAND * PATCH, tile_cols), f32),
            pltpu.VMEM((BAND * tile_cols, PATCH * channels), f32),
            pltpu.VMEM((depth, width), bf16),
            pltpu.VMEM((groups, units * unit, width), f32),
            pltpu.VMEM((layers, groups, units, unit, width), bf16),
            pltpu.VMEM((layers, halo, unit, width), bf16),
            pltpu.VMEM(masks, f32),
            pltpu.VMEM((groups, units * unit, width), bf16),
            pltpu.VMEM((groups + 2, (units + 2) * unit, 2 * width), bf16),
            pltpu.VMEM((layers, 3, width, width), bf16),
            pltpu.VMEM((layers, width, width), bf16),
            pltpu.VMEM((8, blocks), jnp.int32),
            pltpu.VMEM((8, blocks), jnp.int32),
            pltpu.VMEM((strip // group, group * blocks, chunk), bf16),
            pltpu.VMEM((16, n_col * slots), f32),
            pltpu.VMEM((n_row, n_col, slots, chunk), bf16),
            pltpu.VMEM((n_row, n_col, slots, chunk), bf16),
            dma((2,)),
            dma((layers, 4)),
            dma((3,)),
            dma((3,)),
            dma((3, n_row)),
            dma((2,)),
            dma((n_row, parts)),
            dma,
            dma,
            dma((n_row, parts)),
            dma((2,)),
            dma((n_row + 1, bands)),
            dma((n_row + 1,)),
            dma,
            dma,
            dma((layers, 8)),
            dma((layers, 8)),
        ],
        compiler_params=pltpu.CompilerParams(
            vmem_limit_bytes=60 * 2**20, collective_id=0, has_side_effects=True
        ),
        name="whole",
    )(
        scans.reshape(blocks * strip * channels, tile_cols),
        dest.reshape(1, blocks),
        offsets.reshape(1, blocks),
        profile_index.reshape(1, blocks),
        profiles,
        embed_weight,
        attn_gain,
        qkv_weight,
        out_weight,
    )
    return result.reshape(TOK_H, token_cols, width)


def solution(mesh):
    placed = (
        P(("row", "col"), None, None, None),
        P(("row", "col"), None),
        P(("row", "col")),
        P(("row", "col")),
        P(),
        P(),
        P(),
        P(),
        P(),
    )
    return jax.shard_map(
        per_device, mesh=mesh, in_specs=placed, out_specs=P("row", "col", None), check_vma=False
    )
```

```python
import functools

import jax
import jax.numpy as jnp
from jax import lax
from jax.experimental import pallas as pl
from jax.experimental.pallas import tpu as pltpu
from jax.sharding import PartitionSpec as P

HEADS = 16
RADIUS = 4
TOK_H = 32
PATCH = 8
BAND = 8

VMEM = pl.BlockSpec(memory_space=pltpu.VMEM)


def normed(stream, gain_row):
    centre = jnp.mean(stream, -1, keepdims=True)
    spread = jnp.mean(jnp.square(stream - centre), -1, keepdims=True)
    return ((stream - centre) * lax.rsqrt(spread + 1e-05) * gain_row).astype(jnp.bfloat16)


def regroup(token_cols, back=False):
    tokens = BAND * token_cols
    each = BAND * RADIUS
    shape = (tokens, tokens)
    grouped = lax.broadcasted_iota(jnp.int32, shape, 1 if back else 0)
    natural = lax.broadcasted_iota(jnp.int32, shape, 0 if back else 1)
    inner = grouped % each
    source = inner // RADIUS * token_cols + grouped // each * RADIUS + inner % RADIUS
    return (natural == source).astype(jnp.float32).astype(jnp.bfloat16)


def store_band(b, total, stream):
    each = BAND * RADIUS
    at = pl.ds(pl.multiple_of(b * each, each), each)
    for g in range(stream.shape[0]):
        stream[g, at, :] = total[g * each : (g + 1) * each]


def load_band(b, stream):
    each = BAND * RADIUS
    at = pl.ds(pl.multiple_of(b * each, each), each)
    return jnp.concatenate([stream[g, at, :] for g in range(stream.shape[0])], 0)


def store_cells(b, cells, inputs):
    each = BAND * RADIUS
    units = each // inputs.shape[2]
    for g in range(inputs.shape[0]):
        rows = slice(g * each, (g + 1) * each)
        inputs[g, pl.ds(b * units, units)] = cells[rows].reshape(
            units, each // units, cells.shape[1]
        )


def iota(shape, dim):
    return lax.broadcasted_iota(jnp.int32, shape, dim)


def hot(mask):
    return mask.astype(jnp.float32).astype(jnp.bfloat16)


def rows_dot(a, b):
    return lax.dot_general(a, b, (((1,), (1,)), ((), ())), preferred_element_type=jnp.float32)


def exact_dot(a, b):
    return jnp.dot(a, b, precision=lax.Precision.HIGHEST, preferred_element_type=jnp.float32)


def target_of(j, z, n):
    if j == n - 1:
        return z
    low = jnp.where(n - 1 - j > z, n - 1 - j, n - 2 - j)
    high = jnp.where(z > j, j, j + 1)
    return jnp.where(2 * z < n, low, high)


def window_bias(token_cols, sizes, bias):
    win = BAND + 2 * RADIUS
    shape = bias.shape[2:]
    q, k = iota(shape, 0), iota(shape, 1)
    q_row = q % (BAND * RADIUS) // RADIUS
    q_col = q // (BAND * RADIUS) * RADIUS + q % RADIUS
    k_row = k % (win * RADIUS) // RADIUS - RADIUS
    k_col = k // (win * RADIUS) * RADIUS + k % RADIUS - RADIUS
    near = (jnp.abs(k_row - q_row) <= RADIUS) & (jnp.abs(k_col - q_col) <= RADIUS)
    for b in range(bias.shape[0]):
        g_row = lax.axis_index("row") * TOK_H + b * BAND + k_row
        row_in = near & (g_row >= 0) & (g_row < TOK_H * sizes[0])
        for s in range(bias.shape[1]):
            g_col = lax.axis_index("col") * token_cols + s * 2 * RADIUS + k_col
            inside = row_in & (g_col >= 0) & (g_col < token_cols * sizes[1])
            bias[b, s] = jnp.where(inside, 0.0, -1e30)


def whole_kernel(
    sizes, capacity, token_cols, parts,
    scans_hbm, dest, offsets, profile, profiles, embed_hbm, gain, qkv, out_w,
    out_hbm,
    scans, embed, placed, got, weighted, marks_out, marks_in, marks, carried, passed,
    carried_early, passed_early,
    counts_out, counts_in, total, den, image, turned, embed2, stream, xs, xhs, bias, q_ref, kv, w, wo,
    feed_out, feed_in, fed, fed_marks, placed_fed, got_fed,
    out, out_sem, load_sem, w_sem, feed_send, feed_recv, fed_sem, place_sem, got_sem, place_mark_sem, mark_sem, local_sem, pass_sem,
    carry_sem, carry_early_sem, count_out_sem, count_in_sem, send, recv,
):
    n_row, n_col = sizes
    layers = w.shape[0]
    blocks = dest.shape[1]
    profile_count, strip, lanes = profiles.shape
    channels = scans.shape[0] // (blocks * strip)
    slots = strip * capacity
    group = max(1, 16 // capacity)
    chunk = channels * lanes // parts
    tile_rows = TOK_H * PATCH
    keys = n_col * slots
    bands = TOK_H // BAND
    per_part = chunk // lanes
    z, col = lax.axis_index("row"), lax.axis_index("col")
    mesh_ids = pl.DeviceIdType.MESH
    f32, bf16 = jnp.float32, jnp.bfloat16
    width = wo.shape[2]
    head_dim = width // HEADS
    groups, units, unit = xs.shape[1:4]
    own = units * unit
    count = groups * own

    loads = [
        pltpu.make_async_copy(scans_hbm, scans, load_sem.at[0]),
        pltpu.make_async_copy(embed_hbm, embed, load_sem.at[1]),
    ]
    w_loads = [
        [
            pltpu.make_async_copy(
                qkv.at[l, :, n * width : (n + 1) * width], w.at[l, n], w_sem.at[l, n]
            )
            for n in range(3)
        ]
        + [pltpu.make_async_copy(out_w.at[l], wo.at[l], w_sem.at[l, 3])]
        for l in range(layers)
    ]
    for load in loads:
        load.start()

    up, down = z > 0, z < n_row - 1
    west, east = col > 0, col < n_col - 1
    l0 = 2 * groups
    r0 = l0 + units + 2
    end = r0 + units + 2
    where = [
        (-1, 0, up), (1, 0, down), (0, -1, west), (0, 1, east),
        (-1, -1, up & west), (-1, 1, up & east), (1, -1, down & west), (1, 1, down & east),
    ]
    opposite = [1, 0, 3, 2, 7, 6, 5, 4]

    def pieces(l):
        x, xh = xs.at[l], xhs.at[l]
        top, bottom = xh.at[:groups], xh.at[groups : 2 * groups]
        left, right = xh.at[l0 + 1 : r0 - 1], xh.at[r0 + 1 : end - 1]
        return [
            (x.at[:, 0], bottom, top),
            (x.at[:, units - 1], top, bottom),
            (x.at[0], right, left),
            (x.at[groups - 1], left, right),
            (x.at[0, 0], xh.at[end - 1], xh.at[l0]),
            (x.at[groups - 1, 0], xh.at[r0 - 1], xh.at[r0]),
            (x.at[0, units - 1], xh.at[r0], xh.at[r0 - 1]),
            (x.at[groups - 1, units - 1], xh.at[l0], xh.at[end - 1]),
        ]

    def send_halo(l, n, at=None):
        dr, dc, there = where[n]
        source, lands, _ = pieces(l)[n]
        if at is not None:
            source, lands = source.at[at], lands.at[at]

        @pl.when(there)
        def _():
            pltpu.make_async_remote_copy(
                src_ref=source,
                dst_ref=lands,
                send_sem=send.at[l, n],
                recv_sem=recv.at[l, n],
                device_id=(z + dr, col + dc),
                device_id_type=mesh_ids,
            ).start()

    def send_band(l, b):
        per_band = BAND // RADIUS
        at = pl.ds(b * per_band, per_band)
        send_halo(l, 2, at)
        send_halo(l, 3, at)

        @pl.when(jnp.equal(b, 0))
        def _():
            for n in (0, 4, 5):
                send_halo(l, n)

        @pl.when(jnp.equal(b, bands - 1))
        def _():
            for n in (1, 6, 7):
                send_halo(l, n)

    def wait_halo(l):
        for n, (_, _, there) in enumerate(where):
            source, _, here = pieces(l)[n]

            @pl.when(there)
            def _(n=n, source=source, here=here):
                pltpu.make_async_copy(source, source, send.at[l, n]).wait()
                pltpu.make_async_copy(here, here, recv.at[l, opposite[n]]).wait()

    early = carried.shape[2]
    outer = (z == 0) | (z == n_row - 1)
    helper = (z == 1) | (z == n_row - 2) if early < parts else z < 0
    feeder = jnp.where(z == 1, 0, n_row - 1)
    aide = jnp.where(z == 0, 1, n_row - 2)

    def to_aide(source, lands, n):
        return pltpu.make_async_remote_copy(
            src_ref=source,
            dst_ref=lands,
            send_sem=feed_send.at[n],
            recv_sem=feed_recv.at[n],
            device_id=(aide, col),
            device_id_type=mesh_ids,
        )

    barrier = pltpu.get_barrier_semaphore()
    for d in range(1, n_col):
        pl.semaphore_signal(
            barrier, inc=1, device_id=(z, lax.rem(col + d, n_col)), device_id_type=mesh_ids
        )
    for d in range(1, n_row):
        pl.semaphore_signal(
            barrier, inc=1, device_id=(lax.rem(z + d, n_row), col), device_id_type=mesh_ids
        )
    for dr, dc, there in where[4:]:

        @pl.when(there)
        def _(dr=dr, dc=dc):
            pl.semaphore_signal(
                barrier, inc=1, device_id=(z + dr, col + dc), device_id_type=mesh_ids
            )

    for l in range(layers):
        for n, (_, _, there) in enumerate(where):
            here = pieces(l)[n][2]

            @pl.when(jnp.logical_not(there))
            def _(here=here):
                here[...] = jnp.zeros(here.shape, here.dtype)

    dest_row, off_row, prof_row = dest[...], offsets[...], profile[...]
    square = jnp.broadcast_to(dest_row.astype(f32), (blocks, blocks))
    earlier = (square.T == square) & (iota((blocks, blocks), 0) < iota((blocks, blocks), 1))
    rank_row = jnp.sum(earlier.astype(f32), 0, keepdims=True).astype(jnp.int32)

    tile_shape = (n_col * 8, blocks)
    step_row = iota(tile_shape, 0) % 8
    tile = jnp.where(step_row < n_row, step_row * n_col + iota(tile_shape, 0) // 8, -1)
    to_tile = hot(tile == dest_row)
    same = iota((128, blocks), 0) % capacity == rank_row
    for n, what in enumerate((off_row, prof_row)):
        value = jnp.where(same, what + 1, 0).astype(f32).astype(bf16)
        marks_out[:, n * 8 : (n + 1) * 8, :] = rows_dot(to_tile, value).reshape(n_col, 8, 128)

    own_profile = (
        iota((blocks, blocks), 0) == jnp.broadcast_to(prof_row, (blocks, blocks))
    ).astype(f32).T[:, :profile_count]
    loads[0].wait()
    for i in range(strip):
        weight = exact_dot(own_profile, profiles[:, i, :])
        for c in range(channels):
            block_row = scans[pl.ds(i * channels + c, blocks, stride=strip * channels), :]
            at = c % per_part * lanes
            weighted[
                c // per_part,
                i // group,
                i % group * blocks : (i % group + 1) * blocks,
                at : at + lanes,
            ] = (block_row * weight).astype(bf16)

    for load in sum(w_loads, []):
        load.start()
    rows_near = up.astype(jnp.int32) + down.astype(jnp.int32)
    cols_near = west.astype(jnp.int32) + east.astype(jnp.int32)
    pl.semaphore_wait(barrier, n_col - 1 + n_row - 1 + rows_near * cols_near)

    if early < parts:
        feed_out[...] = jnp.broadcast_to(dest_row * (group * capacity) + rank_row, feed_out.shape)

        @pl.when(outer)
        def _():
            to_aide(feed_out, feed_in, 0).start()
            to_aide(weighted.at[early], fed, 1).start()

    slot_row = jnp.concatenate(
        [dest_row * (group * capacity) + ig * capacity + rank_row for ig in range(group)], 1
    )
    per_step = n_col * group * capacity
    for d in range(1, n_col):
        peer = lax.rem(col + d, n_col)
        pltpu.make_async_remote_copy(
            src_ref=marks_out.at[peer],
            dst_ref=marks_in.at[col],
            send_sem=place_mark_sem,
            recv_sem=mark_sem,
            device_id=(z, peer),
            device_id_type=mesh_ids,
        ).start()

    def place(t, pick, source, puts, takes, local, sent, seen):
        for g in range(strip // group):
            y = jnp.dot(pick, source[g], preferred_element_type=f32).astype(bf16)
            puts[:, g * group * capacity : (g + 1) * group * capacity, :] = y.reshape(
                n_col, group * capacity, chunk
            )
        pltpu.make_async_copy(puts.at[col], takes.at[col], local).start()
        for d in range(1, n_col):
            peer = lax.rem(col + d, n_col)
            pltpu.make_async_remote_copy(
                src_ref=puts.at[peer],
                dst_ref=takes.at[col],
                send_sem=sent,
                recv_sem=seen,
                device_id=(z, peer),
                device_id_type=mesh_ids,
            ).start()

    def place_own(j):
        t = target_of(j, z, n_row)
        pick = hot(iota((per_step, group * blocks), 0) + t * per_step == slot_row)
        for h in range(parts):

            def go(h=h):
                place(
                    t, pick, weighted.at[h], placed.at[t, h], got.at[t, h],
                    local_sem.at[j, h], place_sem.at[int(h == early)], got_sem.at[j, h],
                )

            if h == early and j < n_row - 1:
                pl.when(jnp.logical_not(outer))(go)
            else:
                go()

    def place_fed(j):
        t = target_of(j, z, n_row)

        @pl.when(helper & (t != feeder))
        def _():
            row = feed_in[0:1, :]
            fed_row = jnp.concatenate([row + ig * capacity for ig in range(group)], 1)
            pick = hot(iota((per_step, group * blocks), 0) + t * per_step == fed_row)
            place(
                t, pick, fed, placed_fed.at[t], got_fed.at[t],
                fed_sem.at[0, j], fed_sem.at[1, 0], fed_sem.at[2, j],
            )

    def await_fed(n, lands):
        @pl.when(helper)
        def _():
            pltpu.make_async_copy(lands, lands, feed_recv.at[n]).wait()

    for j in range(n_row):
        place_own(j)
        if early < parts and j == 1:
            await_fed(0, feed_in)
            await_fed(1, fed)
            place_fed(0)
            place_fed(1)
        if early < parts and j > 1:
            place_fed(j)

    def prepare():
        loads[1].wait()
        depth = embed.shape[0]
        pick_shape = (depth, depth)
        inner = depth // PATCH
        source = iota(pick_shape, 0) % inner * PATCH + iota(pick_shape, 0) // inner
        reorder = hot(iota(pick_shape, 1) == source)
        for n in range(0, embed.shape[1], 512):
            embed2[:, n : n + 512] = jnp.dot(
                reorder, embed[:, n : n + 512], preferred_element_type=f32
            ).astype(bf16)
        window_bias(token_cols, sizes, bias)

    def denominator():
        pltpu.make_async_copy(
            counts_in.at[: n_row - 1], counts_in.at[: n_row - 1], count_in_sem
        ).wait()
        hits = counts_in[0].astype(f32)
        for s in range(1, n_row):
            hits += counts_in[s].astype(f32)
        divisor = jnp.ones((tile_rows, lanes), f32)
        for i in range(strip):
            shifted = hits if i == 0 else pltpu.roll(hits, i, 1)
            divisor += exact_dot(shifted.T, profiles[:, i, :])
        den[...] = divisor

    part_tokens = BAND * token_cols
    order = regroup(token_cols)
    prepare()
    band_rows = BAND * PATCH

    def embed_band(k):
        rows = slice(k * band_rows, (k + 1) * band_rows)
        for c in range(channels):
            at = c % per_part * lanes
            pixels = total[(n_row - 1) % 2, c // per_part, rows, at : at + lanes] / den[rows, :]
            image[c] = pixels.astype(bf16).astype(f32)
        for i in range(BAND):
            block = image[:, i * PATCH : (i + 1) * PATCH, :].reshape(channels * PATCH, lanes)
            turned[i * lanes : (i + 1) * lanes, :] = block.T
        lhs = jnp.concatenate(
            [turned[pl.ds(q, part_tokens, stride=PATCH), :] for q in range(PATCH)], 1
        ).astype(bf16)
        lhs = jnp.dot(order, lhs, preferred_element_type=f32).astype(bf16)
        cells = jnp.dot(lhs, embed2[...], preferred_element_type=f32)
        store_band(k, cells, stream)
        store_cells(k, normed(cells, gain[0:1, :]), xs.at[0])
        send_band(0, k)

    pltpu.make_async_copy(
        marks_in.at[: n_col - 1], marks_in.at[: n_col - 1], mark_sem
    ).wait()
    per_tile = 128 // slots
    for u in range(keys // 128):
        mark = jnp.zeros((16, 128), f32)
        for s in range(per_tile):
            src = u * per_tile + s
            seen = jnp.where(src == col, marks_out[src], marks_in[src])
            mark = jnp.where(iota((16, 128), 1) // slots == s, seen, mark)
        marks[:, u * 128 : (u + 1) * 128] = mark
    if early < parts:

        @pl.when(outer)
        def _():
            to_aide(marks, fed_marks, 2).start()

        await_fed(2, fed_marks)
    strip_row = iota((1, keys), 1) % slots // capacity
    pixel = iota((tile_rows, keys), 0)

    def spread_of(table, t):
        mark = table[pl.ds(t, 1), :].astype(jnp.int32)
        return hot(pixel == jnp.where(mark > 0, mark - 1 + strip_row, -1))

    def count_of(j):
        t = target_of(j, z, n_row)
        first = jnp.where(strip_row == 0, marks[pl.ds(t + 8, 1), :].astype(jnp.int32), 0)
        by_profile = hot(iota((profile_count, keys), 0) + 1 == first)
        hits = rows_dot(by_profile, spread_of(marks, t)).astype(bf16)
        if j == n_row - 1:
            counts_in[z] = hits
            return
        counts_out[t] = hits
        pltpu.make_async_remote_copy(
            src_ref=counts_out.at[t],
            dst_ref=counts_in.at[z],
            send_sem=count_out_sem,
            recv_sem=count_in_sem,
            device_id=(t, col),
            device_id_type=mesh_ids,
        ).start()

    def gather(j, part_list):
        t = target_of(j, z, n_row)
        spread = spread_of(marks, t)
        for h in part_list:
            pltpu.make_async_copy(
                placed.at[t, h, col], got.at[t, h, col], local_sem.at[j, h]
            ).wait()
            pltpu.make_async_copy(
                got.at[t, h, : n_col - 1], got.at[t, h, : n_col - 1], got_sem.at[j, h]
            ).wait()
            total[j % 2, h] = jnp.dot(
                spread, got[t, h].reshape(keys, chunk), preferred_element_type=f32
            )
            if h == early:

                @pl.when(helper & (t != feeder))
                def _():
                    pltpu.make_async_copy(
                        placed_fed.at[t, col], got_fed.at[t, col], fed_sem.at[0, j]
                    ).wait()
                    some = got_fed.at[t, : n_col - 1]
                    pltpu.make_async_copy(some, some, fed_sem.at[2, j]).wait()
                    total[j % 2, early] += jnp.dot(
                        spread_of(fed_marks, t),
                        got_fed[t].reshape(keys, chunk),
                        preferred_element_type=f32,
                    )

    def add(there, j, here, r):
        @pl.when(there)
        def _():
            if r is None:
                lands = carried_early.at[here]
                pltpu.make_async_copy(lands, lands, carry_early_sem.at[here]).wait()
                total[j % 2, early] += carried_early[here].astype(f32)
            else:
                lands = carried.at[here, r]
                pltpu.make_async_copy(lands, lands, carry_sem.at[here, r]).wait()
                rows = slice(r * band_rows, (r + 1) * band_rows)
                total[j % 2, :early, rows, :] += carried[here, r].astype(f32)

    def forward(j, r):
        t = target_of(j, z, n_row)
        above = t > z
        near = jnp.where(above, z + 1, z - 1)
        slot = jnp.where(jnp.logical_not(above) & (near == t), n_row, t)
        margin = int(r is None)
        add(jnp.where(above, z > margin, z < n_row - 1 - margin), j, t, r)
        if r is None:
            passed_early[t] = total[j % 2, early].astype(bf16)
            source, lands = passed_early.at[t], carried_early.at[slot]
            sems = pass_sem.at[1], carry_early_sem.at[slot]
        else:
            passed[t, r] = total[j % 2, :early, r * band_rows : (r + 1) * band_rows, :].astype(bf16)
            source, lands = passed.at[t, r], carried.at[slot, r]
            sems = pass_sem.at[0], carry_sem.at[slot, r]
        pltpu.make_async_remote_copy(
            src_ref=source,
            dst_ref=lands,
            send_sem=sems[0],
            recv_sem=sems[1],
            device_id=(near, col),
            device_id_type=mesh_ids,
        ).start()

    def forward_early(j):
        if early < parts:

            @pl.when(jnp.logical_not(outer))
            def _():
                gather(j, [early])
                forward(j, None)

    band_order = [0, bands - 1, *range(1, bands - 1)]
    for j in range(n_row):
        count_of(j)
    pairs = [list(range(j, min(j + 2, n_row - 1))) for j in range(1, n_row - 1, 2)]
    for js in [[0], *pairs]:
        for r in band_order:
            for j in js:
                if r == 0:
                    gather(j, range(early))
                forward(j, r)
            if r == (band_order[-1] if js == [0] else 0):
                for j in js:
                    forward_early(j)
    final = n_row - 1
    denominator()
    gather(final, range(early))
    if early < parts:
        gather(final, [early])
        add(z > 1, final, z, None)
        add(z < n_row - 2, final, n_row, None)
    for r in band_order:
        add(z > 0, final, z, r)
        add(z < n_row - 1, final, n_row, r)
        embed_band(r)

    step = 1024

    def project(rows, weight, put):
        def part(k, c):
            cols = pl.ds(pl.multiple_of(k * step, step), step)
            y = jnp.dot(
                rows[...].reshape(-1, width), weight[:, cols], preferred_element_type=f32
            ).astype(bf16)
            put(k, y)
            return c

        lax.fori_loop(0, width // step, part, 0)

    def put_q(k, y):
        cols = pl.ds(pl.multiple_of(k * step, step), step)
        for g in range(groups):
            q_ref[g, :, cols] = (y[g * own : (g + 1) * own] * head_dim ** (-0.5)).astype(
                jnp.bfloat16
            )

    def put_own(base, k, y):
        cols = pl.ds(pl.multiple_of(base + k * step, step), step)
        for g in range(groups):
            kv[g + 1, unit : unit + own, cols] = y[g * own : (g + 1) * own]

    def put_halo(base, k, y):
        cols = pl.ds(pl.multiple_of(base + k * step, step), step)
        for g in range(groups):
            kv[g + 1, :unit, cols] = y[g * unit : (g + 1) * unit]
            kv[g + 1, unit + own :, cols] = y[(groups + g) * unit : (groups + g + 1) * unit]
        kv[0, :, cols] = y[l0 * unit : r0 * unit]
        kv[groups + 1, :, cols] = y[r0 * unit :]

    each = BAND * RADIUS
    span = (BAND + 2 * RADIUS) * RADIUS
    pair = 2 * head_dim
    queries = 2 * each
    low = lax.broadcasted_iota(jnp.int32, (queries, pair), 1) < head_dim
    ones = jnp.ones((4 * span, pair), jnp.bfloat16)
    back = regroup(token_cols, True)

    def band(l, n, carry):
        last = l == layers - 1
        b = n if last else jnp.where(n == 0, 0, jnp.where(n == 1, bands - 1, n - 1))
        q_at = pl.ds(pl.multiple_of(b * each, each), each)
        k_at = pl.ds(pl.multiple_of(b * each, each), span)
        halves = []
        for s in range(groups // 2):
            half_bias = bias[b, s]
            both = jnp.concatenate([half_bias, half_bias], 0)
            pieces = []
            for h in range(HEADS // 2):
                cols = slice(h * pair, (h + 1) * pair)
                v_cols = slice(width + h * pair, width + (h + 1) * pair)
                q = jnp.concatenate([q_ref[2 * s + i, q_at, cols] for i in range(2)], 0)
                zero = jnp.zeros_like(q)
                q2 = jnp.concatenate([jnp.where(low, q, zero), jnp.where(low, zero, q)], 0)
                k = jnp.concatenate([kv[2 * s + i, k_at, cols] for i in range(4)], 0)
                v = jnp.concatenate([kv[2 * s + i, k_at, v_cols] for i in range(4)], 0)
                logits = lax.dot_general(
                    q2, k, (((1,), (1,)), ((), ())), preferred_element_type=jnp.float32
                )
                logits = logits + both
                top_logit = jnp.max(logits, -1, keepdims=True)
                weight = jnp.exp(logits - top_logit).astype(jnp.bfloat16)
                summed = jnp.dot(
                    weight, jnp.concatenate([v, ones], 1), preferred_element_type=jnp.float32
                )
                share = summed[:, :pair] / summed[:, pair:]
                pieces.append(
                    jnp.where(low, share[:queries], share[queries:]).astype(jnp.bfloat16)
                )
            halves.append(jnp.concatenate(pieces, 1))
        attended = jnp.concatenate(halves, 0)
        summed = load_band(b, stream) + jnp.dot(attended, wo[l], preferred_element_type=f32)
        if last:
            rows = BAND * token_cols
            out[pl.ds(pl.multiple_of(b * rows, rows), rows), :] = jnp.dot(
                back, summed.astype(jnp.bfloat16), preferred_element_type=jnp.float32
            ).astype(jnp.bfloat16)
            done = pl.ds(pl.multiple_of(b * rows, rows), rows)
            pltpu.make_async_copy(out.at[done], out_hbm.at[done], out_sem).start()
        else:
            store_band(b, summed, stream)
            store_cells(b, normed(summed, gain[l + 1 : l + 2, :]), xs.at[l + 1])
            send_band(l + 1, b)
        return carry

    for l in range(layers):
        for n in range(3):
            w_loads[l][n].wait()
            put = put_q if n == 0 else functools.partial(put_own, (n - 1) * width)
            project(xs.at[l], w.at[l, n], put)
        wait_halo(l)
        for n in (1, 2):
            project(xhs.at[l], w.at[l, n], functools.partial(put_halo, (n - 1) * width))
        w_loads[l][3].wait()
        lax.fori_loop(0, bands, functools.partial(band, l), 0)

    pltpu.make_async_copy(out, out_hbm, out_sem).wait()
    for src, sem in (
        (marks_out.at[: n_col - 1], place_mark_sem),
        (placed.at[:, :early, : n_col - 1], place_sem.at[0]),
        (counts_out.at[: n_row - 1], count_out_sem),
        (passed.at[: n_row - 1], pass_sem.at[0]),
    ):
        pltpu.make_async_copy(src, src, sem).wait()
    if early < parts:

        @pl.when(outer)
        def _():
            to_aide(feed_out, feed_in, 0).wait_send()
            to_aide(weighted.at[early], fed, 1).wait_send()
            to_aide(marks, fed_marks, 2).wait_send()
            sent = placed.at[0, early, : n_col - 1]
            pltpu.make_async_copy(sent, sent, place_sem.at[1]).wait()

        @pl.when(jnp.logical_not(outer))
        def _():
            for src, sem in (
                (placed.at[:, early, : n_col - 1], place_sem.at[1]),
                (passed_early.at[: n_row - 1], pass_sem.at[1]),
            ):
                pltpu.make_async_copy(src, src, sem).wait()

        @pl.when(helper)
        def _():
            sent = placed_fed.at[: n_row - 1, : n_col - 1]
            pltpu.make_async_copy(sent, sent, fed_sem.at[1, 0]).wait()


def per_device(
    scans, dest, offsets, profile_index, profiles, embed_weight, attn_gain, qkv_weight, out_weight
):
    sizes = (lax.axis_size("row"), lax.axis_size("col"))
    n_row, n_col = sizes
    blocks, strip, channels, tile_cols = scans.shape
    token_cols = tile_cols // PATCH
    count = TOK_H * token_cols
    tile_rows = TOK_H * PATCH
    profile_count = profiles.shape[0]
    depth, width = embed_weight.shape
    layers = qkv_weight.shape[0]
    capacity = max(2, 2 * blocks // (n_row * n_col))
    capacity = -(-capacity * strip // 16) * 16 // strip
    slots = strip * capacity
    group = max(1, 16 // capacity)
    parts = 4
    dense = parts - 1 if n_row > 3 else parts
    bands = TOK_H // BAND
    chunk = channels * tile_cols // parts
    f32, bf16 = jnp.float32, jnp.bfloat16

    groups = token_cols // RADIUS
    unit = RADIUS * RADIUS
    units = TOK_H // RADIUS
    halo = 2 * groups + 2 * (units + 2)
    win = BAND + 2 * RADIUS
    masks = (TOK_H // BAND, token_cols // (2 * RADIUS), 2 * BAND * RADIUS, 4 * win * RADIUS)
    dma = pltpu.SemaphoreType.DMA
    hbm = pl.BlockSpec(memory_space=pl.ANY)
    result = pl.pallas_call(
        functools.partial(whole_kernel, sizes, capacity, token_cols, parts),
        out_shape=jax.ShapeDtypeStruct((count, width), bf16),
        in_specs=[hbm, VMEM, VMEM, VMEM, VMEM, hbm, VMEM, hbm, hbm],
        out_specs=hbm,
        scratch_shapes=[
            pltpu.VMEM((blocks * strip * channels, tile_cols), f32),
            pltpu.VMEM((depth, width), bf16),
            pltpu.VMEM((n_row, parts, n_col, slots, chunk), bf16),
            pltpu.VMEM((n_row, parts, n_col, slots, chunk), bf16),
            pltpu.VMEM((parts, strip // group, group * blocks, chunk), bf16),
            pltpu.VMEM((n_col, 16, 128), f32),
            pltpu.VMEM((n_col, 16, 128), f32),
            pltpu.VMEM((16, n_col * slots), f32),
            pltpu.VMEM((n_row + 1, bands, dense, BAND * PATCH, chunk), bf16),
            pltpu.VMEM((n_row, bands, dense, BAND * PATCH, chunk), bf16),
            pltpu.VMEM((n_row + 1, tile_rows, chunk), bf16),
            pltpu.VMEM((n_row, tile_rows, chunk), bf16),
            pltpu.VMEM((n_row, profile_count, tile_rows), bf16),
            pltpu.VMEM((n_row, profile_count, tile_rows), bf16),
            pltpu.VMEM((2, parts, tile_rows, chunk), f32),
            pltpu.VMEM((tile_rows, tile_cols), f32),
            pltpu.VMEM((channels, BAND * PATCH, tile_cols), f32),
            pltpu.VMEM((BAND * tile_cols, PATCH * channels), f32),
            pltpu.VMEM((depth, width), bf16),
            pltpu.VMEM((groups, units * unit, width), f32),
            pltpu.VMEM((layers, groups, units, unit, width), bf16),
            pltpu.VMEM((layers, halo, unit, width), bf16),
            pltpu.VMEM(masks, f32),
            pltpu.VMEM((groups, units * unit, width), bf16),
            pltpu.VMEM((groups + 2, (units + 2) * unit, 2 * width), bf16),
            pltpu.VMEM((layers, 3, width, width), bf16),
            pltpu.VMEM((layers, width, width), bf16),
            pltpu.VMEM((8, blocks), jnp.int32),
            pltpu.VMEM((8, blocks), jnp.int32),
            pltpu.VMEM((strip // group, group * blocks, chunk), bf16),
            pltpu.VMEM((16, n_col * slots), f32),
            pltpu.VMEM((n_row, n_col, slots, chunk), bf16),
            pltpu.VMEM((n_row, n_col, slots, chunk), bf16),
            pltpu.VMEM((count, width), bf16),
            dma,
            dma((2,)),
            dma((layers, 4)),
            dma((3,)),
            dma((3,)),
            dma((3, n_row)),
            dma((2,)),
            dma((n_row, parts)),
            dma,
            dma,
            dma((n_row, parts)),
            dma((2,)),
            dma((n_row + 1, bands)),
            dma((n_row + 1,)),
            dma,
            dma,
            dma((layers, 8)),
            dma((layers, 8)),
        ],
        compiler_params=pltpu.CompilerParams(
            vmem_limit_bytes=60 * 2**20, collective_id=0, has_side_effects=True
        ),
        name="whole",
    )(
        scans.reshape(blocks * strip * channels, tile_cols),
        dest.reshape(1, blocks),
        offsets.reshape(1, blocks),
        profile_index.reshape(1, blocks),
        profiles,
        embed_weight,
        attn_gain,
        qkv_weight,
        out_weight,
    )
    return result.reshape(TOK_H, token_cols, width)


def solution(mesh):
    placed = (
        P(("row", "col"), None, None, None),
        P(("row", "col"), None),
        P(("row", "col")),
        P(("row", "col")),
        P(),
        P(),
        P(),
        P(),
        P(),
    )
    return jax.shard_map(
        per_device, mesh=mesh, in_specs=placed, out_specs=P("row", "col", None), check_vma=False
    )
```
